128 devices in a mesh: walker: 32 (over x, z, core), owner: 4 (over y).
Axes of the slice: x: 4, y: 4, z: 4, core: 2. Of those that a mesh axis runs over, the one named last changes fastest.
Arguments:
- block_input_rows: bfloat16 [2048, 1024, 256], P(('walker', 'owner')), may hold values from -6 to 6
- spin_values: int32 [2048, 1024], P(('walker', 'owner')), may hold values 0 or 1
- conv_weight: bfloat16 [256, 512], replicated, may hold values from -0.25 to 0.25
- conv_bias: float32 [256], replicated, may hold values from -3 to 3
- readout: float32 [256], replicated, may hold values from -0.375 to 0.375
- energies: float32 [2048], P(('walker', 'owner')), may hold values from -1 to 0.1
- basis_out: bfloat16 [256, 256], P(None, 'owner'), may hold values from -0.375 to 0.375
- basis_in: bfloat16 [512, 512], P(None, 'owner'), may hold values from -6 to 6
Outputs:
- moment_stats: float32 [256, 512], P(None, 'owner')
- update: float32 [256, 512], P(None, 'owner')
The draws below stay inside these ranges and needn't reach their ends.
All inputs are finite; a program needn't handle non-finite values. No bound on the sum of `spin_values` on one device may be relied on, other than what follows from the above.
Results may differ from the reference program's by a relative error of at most 0.025.
Values may be sent and summed in bfloat16 or wider, within the bound.
A program may use at most 128 MiB of HBM per device.

```python
import jax
import jax.numpy as jnp
from jax import lax

CONV_CHANNELS = 256
CHAIN_SITES = 1024
DILATION_STEP = 16
SAMPLES = 2048


def draw_energies(key, part):
    position = jnp.arange(SAMPLES).astype(jnp.float32)
    trend = -0.443 * (0.5 + position / (SAMPLES - 1))
    noise = 0.1 * jax.random.truncated_normal(key, -3.0, 3.0, (SAMPLES,), jnp.float32)
    return jnp.clip(trend + noise, -1.0, 0.1).astype(jnp.float32)


def draw_basis_in(key, part):
    width = 2 * CONV_CHANNELS
    row_pos = jnp.arange(width).astype(jnp.float32) / (width - 1)
    entries = jax.random.truncated_normal(key, -4.0, 4.0, (width, width), jnp.float32)
    row_scale = jnp.exp(jnp.log(10.0) * row_pos)
    values = entries * row_scale[:, None] / jnp.sqrt(jnp.float32(width)) * 5.0
    return jnp.clip(values, -6.0, 6.0).astype(jnp.bfloat16)


def with_ends(result, rng, low, high):
    place = [jax.random.randint(jax.random.fold_in(rng, axis), (), 0, length) for axis, length in enumerate(result.shape)]
    main_axis = result.shape.index(max(result.shape))
    beside = place[:main_axis] + [(place[main_axis] + 1) % result.shape[main_axis]] + place[main_axis + 1:]
    return result.at[tuple(place)].set(low).at[tuple(beside)].set(high)


def steps_of(stream_key, dims, cuts, least, top_value):
    factor_of, own = 1.0, jax.random.fold_in(stream_key, 6)
    for dim, parts in cuts:
        heights = jnp.exp(jax.random.uniform(jax.random.fold_in(own, dim), (parts,), jnp.float32, least / len(cuts), top_value / len(cuts)))
        factor_of = factor_of * jnp.repeat(heights, dims[dim] // parts).reshape([-1 if axis == dim else 1 for axis in range(len(dims))])
    return factor_of


def centred(own_key, dims, scale, reach, shards=(), kind=jnp.bfloat16):
    result = scale * jax.random.normal(own_key, dims, jnp.float32)
    if shards:
        result = result * steps_of(own_key, dims, shards, -0.22, 0.18)
    return jnp.clip(result, -reach, reach).astype(kind)


def setup_inputs(seed: int = 0) -> dict:
    keys = jax.random.split(jax.random.key(seed), 9)
    block_input_rows = centred(keys[0], (SAMPLES, CHAIN_SITES, CONV_CHANNELS), 1.0, 6.0, ((0, 128),))
    spin_values = with_ends((jax.random.randint(keys[1], (SAMPLES, CHAIN_SITES), 0, 2) < 1).astype(jnp.int32), jax.random.fold_in(keys[1], 1), 0, 1)
    conv_weight = centred(keys[2], (CONV_CHANNELS, 2 * CONV_CHANNELS), (2 * CONV_CHANNELS) ** -0.5, 0.25)
    conv_bias = centred(keys[3], (CONV_CHANNELS,), 0.5, 3.0, (), jnp.float32)
    readout = centred(keys[4], (CONV_CHANNELS,), CONV_CHANNELS ** -0.5, 0.375, (), jnp.float32)
    energies = draw_energies(jax.random.fold_in(keys[8], 71), 0)
    basis_out = centred(keys[6], (CONV_CHANNELS, CONV_CHANNELS), CONV_CHANNELS ** -0.5, 0.375, ((1, 4),))
    basis_in = draw_basis_in(jax.random.fold_in(keys[8], 71), 0)
    return dict(block_input_rows=block_input_rows, spin_values=spin_values, conv_weight=conv_weight, conv_bias=conv_bias, readout=readout, energies=energies, basis_out=basis_out, basis_in=basis_in)


DAMPING = 0.01

def sample_projection(sample_row_block, spin_row, conv_weight, conv_bias, readout, basis_out, basis_in):
    now_part = jnp.dot(sample_row_block, conv_weight[:, CONV_CHANNELS:].T, preferred_element_type=jnp.float32)
    earlier_portion = jnp.dot(sample_row_block, conv_weight[:, :CONV_CHANNELS].T, preferred_element_type=jnp.float32)
    delayed_input = jnp.concatenate([jnp.zeros((DILATION_STEP, CONV_CHANNELS), jnp.float32), earlier_portion[:CHAIN_SITES - DILATION_STEP]], axis=0)
    pre_act = now_part + delayed_input + conv_bias
    activation = jnp.tanh(pre_act)
    logit_rows = lax.optimization_barrier(jnp.sum((sample_row_block.astype(jnp.float32) + activation) * readout, axis=-1))
    target = spin_row.astype(jnp.float32)
    backward_signal = (0.5 * (target - jax.nn.sigmoid(logit_rows)))[:, None] * readout[None, :] * (1.0 - activation * activation)
    backward_signal = backward_signal.astype(jnp.bfloat16)
    grad_now = jnp.dot(backward_signal.T, sample_row_block, preferred_element_type=jnp.float32)
    gradient_earlier = jnp.dot(backward_signal[DILATION_STEP:].T, sample_row_block[:CHAIN_SITES - DILATION_STEP], preferred_element_type=jnp.float32)
    gradient = jnp.concatenate([gradient_earlier, grad_now], axis=1).astype(jnp.bfloat16)
    half_proj = jnp.dot(basis_out.T, gradient, preferred_element_type=jnp.float32).astype(jnp.bfloat16)
    return jnp.dot(half_proj, basis_in, preferred_element_type=jnp.float32)

def reference(block_input_rows, spin_values, conv_weight, conv_bias, readout, energies, basis_out, basis_in):
    energy_mean = jnp.sum(energies) / SAMPLES
    energy_coeff = energies - energy_mean

    def accumulate(running, inputs):
        squares, weighted = running
        sample_row_block, spin_row, coeff_value = inputs
        projected = sample_projection(sample_row_block, spin_row, conv_weight, conv_bias, readout, basis_out, basis_in)
        return ((squares + projected * projected, weighted + coeff_value * projected), None)
    zeros_init = jnp.zeros((CONV_CHANNELS, 2 * CONV_CHANNELS), jnp.float32)
    (squares, weighted), _ = lax.scan(accumulate, (zeros_init, zeros_init), (block_input_rows, spin_values, energy_coeff))
    moment_stats = squares / SAMPLES
    scaled_ratio = (weighted / SAMPLES / (moment_stats + DAMPING)).astype(jnp.bfloat16)
    mixed_basis = jnp.dot(basis_out, scaled_ratio, preferred_element_type=jnp.float32).astype(jnp.bfloat16)
    raw_update = jnp.dot(mixed_basis, basis_in.T, preferred_element_type=jnp.float32)
    mean_sq = jnp.sum(raw_update * raw_update) / (CONV_CHANNELS * 2 * CONV_CHANNELS)
    return (moment_stats, raw_update / jnp.sqrt(mean_sq + 1e-06))
```

```python
import jax
import jax.numpy as jnp
from jax import lax
from jax.experimental import pallas as pl
from jax.experimental.pallas import tpu as pltpu
from jax.sharding import PartitionSpec as P

DILATION_STEP = 16
DAMPING = 0.01
BF = jnp.bfloat16
F32 = jnp.float32
MESH = pl.DeviceIdType.MESH

GROUPS = 16
OWNERS = 4
LANES = 128


def dot_nt(a, b):
    return lax.dot_general(a, b, (((1,), (1,)), ((), ())), preferred_element_type=F32)


def dot_nn(a, b):
    return jnp.dot(a, b, preferred_element_type=F32)


def wide(value, count):
    return jnp.concatenate([value] * count, axis=1) if count > 1 else value


def kernel(
    x_hbm, spin_ref, w_ref, bias_ref, readout_ref, e_ref, bo_ref, bi_ref,
    stats_ref, update_ref,
    xbuf, back, grads, halves, bo_full, bi_full, bias_col, read_col, read_rows,
    e_out, e_in, core_out, core_in, own, y_out, y_in, plane_out, plane_in, plane_own,
    ring, ratio_full, stats_out, stats_in, raw_buf,
    x_sem, basis_send, basis_recv, e_send, e_recv, core_send, core_recv,
    y_send, y_recv, plane_send, plane_recv, ring_send, ring_recv, last_send, last_recv,
):
    samples, sites, channels = x_hbm.shape
    pad = DILATION_STEP
    total_samples = samples * 128
    walker = lax.axis_index("walker")
    owner = lax.axis_index("owner")
    core = lax.rem(walker, 2)
    group = walker // 2
    gx, gz = group // 4, lax.rem(group, 4)
    twin = (group * 2 + (1 - core), owner)

    def across(step):
        return (walker, lax.rem(owner + step, OWNERS))

    def plane(dx, dz):
        return lax.rem(gx + dx, 4) * 4 + lax.rem(gz + dz, 4)

    def plane_id(dx, dz):
        return (plane(dx, dz) * 2 + core, owner)

    plane_steps = [(k // 4, k % 4) for k in range(1, GROUPS)]
    peers = [twin] + [across(d) for d in (1, 2, 3)] + [plane_id(*s) for s in plane_steps]

    barrier = pltpu.get_barrier_semaphore()
    for peer in peers:
        pl.semaphore_signal(barrier, inc=1, device_id=peer, device_id_type=MESH)

    def load(i):
        return pltpu.make_async_copy(x_hbm.at[i], xbuf.at[i, pl.ds(pad, sites), :], x_sem.at[i])

    for i in range(samples):
        load(i).start()

    def send(src, dst, ssem, rsem, peer):
        return pltpu.make_async_remote_copy(
            src_ref=src, dst_ref=dst, send_sem=ssem, recv_sem=rsem,
            device_id=peer, device_id_type=MESH,
        )

    bias_col[...] = jnp.broadcast_to(bias_ref[...], (LANES, channels)).T
    read_col[...] = jnp.broadcast_to(readout_ref[...], (LANES, channels)).T
    r = readout_ref[...]
    hi = r.astype(BF).astype(F32)
    mid = (r - hi).astype(BF).astype(F32)
    low = r - hi - mid
    row = lax.broadcasted_iota(jnp.int32, (16, channels), 0)
    spread = jnp.where(row == 0, hi, jnp.where(row == 1, mid, jnp.where(row == 2, low, 0.0)))
    read_rows[...] = spread.astype(BF)
    for i in range(samples):
        xbuf[i, 0:pad, :] = jnp.zeros((pad, channels), BF)

    own_rows = pl.ds(pl.multiple_of(owner * 64, 64), 64)
    own_cols = pl.ds(pl.multiple_of(owner * LANES, LANES), LANES)
    bo_full[own_rows, :] = bo_ref[...]
    bi_full[:, own_cols] = bi_ref[...]

    def basis_copies():
        out = []
        for d in (1, 2, 3):
            out.append(send(bo_ref, bo_full.at[own_rows, :], basis_send.at[d - 1],
                            basis_recv.at[d - 1], across(d)))
            out.append(send(bi_ref, bi_full.at[:, own_cols], basis_send.at[d + 2],
                            basis_recv.at[d + 2], across(d)))
        return out

    e_sum = e_ref[0]
    for i in range(1, samples):
        e_sum = e_sum + e_ref[i]
    e_out[0] = jnp.full((8, LANES), e_sum, F32)
    stages = [
        [twin],
        [across(d) for d in (1, 2, 3)],
        [plane_id(d, 0) for d in (1, 2, 3)],
        [plane_id(0, d) for d in (1, 2, 3)],
    ]
    first_slot = [0, 1, 4, 7]

    def energy_copies(stage):
        base = first_slot[stage]
        return [send(e_out.at[stage], e_in.at[base + k], e_send.at[base + k],
                     e_recv.at[base + k], peer) for k, peer in enumerate(stages[stage])]

    def energy_finish(stage):
        copies = energy_copies(stage)
        for c in copies:
            c.wait()
        total = e_out[stage]
        for k in range(len(copies)):
            total = total + e_in[first_slot[stage] + k]
        e_out[stage + 1] = total

    chunk = 256

    @pl.loop(0, samples)
    def _(i):
        @pl.when(i == 1)
        def _():
            pl.semaphore_wait(barrier, len(peers))
            for c in energy_copies(0):
                c.start()
            for c in basis_copies():
                c.start()

        for stage in range(4):
            @pl.when(i == 4 + 3 * stage)
            def _(stage=stage):
                energy_finish(stage)
                if stage < 3:
                    for c in energy_copies(stage + 1):
                        c.start()

        load(i).wait()
        for c in range(sites // chunk):
            lo = c * chunk
            x_prev = xbuf[i, lo:lo + chunk, :]
            x_now = xbuf[i, lo + pad:lo + pad + chunk, :]
            pre = dot_nt(w_ref[:, :channels], x_prev) + dot_nt(w_ref[:, channels:], x_now)
            x_logit = dot_nt(read_rows[...], x_now)
            act = jnp.tanh(pre + wide(bias_col[...], chunk // LANES))
            logit = jnp.sum(act * wide(read_col[...], chunk // LANES), axis=0, keepdims=True)
            logit = logit + jnp.sum(x_logit, axis=0, keepdims=True)
            target = spin_ref[pl.ds(i, 1), lo:lo + chunk].astype(F32)
            signal = 0.5 * (target - jax.nn.sigmoid(logit))
            back[:, lo:lo + chunk] = (signal * (1.0 - act * act)).astype(BF)
        scale = wide(read_col[...], channels // LANES)
        b = back[...]
        grads[i, :, :channels] = (dot_nn(b, xbuf[i, :sites, :]) * scale).astype(BF)
        grads[i, :, channels:] = (dot_nn(b, xbuf[i, pad:, :]) * scale).astype(BF)

    for c in basis_copies():
        c.wait()

    @pl.loop(0, samples)
    def _(i):
        halves[i] = dot_nn(bo_full[...], grads[i]).astype(BF)

    e_mean = jnp.broadcast_to(e_out[4][0:1, :], (64, LANES)) * (1.0 / total_samples)

    def project(first, tile):
        q, m = tile // 2, tile % 2
        rows = pl.ds(pl.multiple_of(first + q * 64, 64), 64)
        lhs = halves[:, rows, :].reshape(samples * 64, 2 * channels)
        p = dot_nn(lhs, bi_full[:, m * 256:(m + 1) * 256])
        squares = jnp.zeros((64, 256), F32)
        weighted = jnp.zeros((64, 256), F32)
        for n in range(samples):
            pn = p[n * 64:(n + 1) * 64]
            squares = squares + pn * pn
            weighted = weighted + pn * wide(e_ref[n] - e_mean, 2)
        out = []
        for k in range(2):
            cols = slice(k * LANES, (k + 1) * LANES)
            out.append((2 * m + k, q * 8, jnp.concatenate(
                [squares[:, cols].reshape(8, 8, LANES), weighted[:, cols].reshape(8, 8, LANES)],
                axis=1)))
        return out

    for tile in range(4):
        for o, g, block in project((1 - core) * 128, tile):
            core_out[o, g:g + 8] = block.astype(BF)
    core_copy = send(core_out, core_in, core_send, core_recv, twin)
    core_copy.start()
    for tile in range(4):
        for o, g, block in project(core * 128, tile):
            own[o, g:g + 8] = block
    core_copy.wait()

    y_copies = []
    for d in (1, 2, 3):
        o = lax.rem(owner + d, OWNERS)
        y_out[d - 1] = (own[o] + core_in[o].astype(F32)).astype(BF)
        y_copies.append(send(y_out.at[d - 1], y_in.at[d - 1], y_send.at[d - 1],
                             y_recv.at[d - 1], across(d)))
        y_copies[-1].start()
    total = own[owner] + core_in[owner].astype(F32)
    for d in (1, 2, 3):
        y_copies[d - 1].wait()
        total = total + y_in[d - 1].astype(F32)

    plane_own[...] = total
    plane_out[...] = total.astype(BF)
    plane_copies = []
    for k, step in enumerate(plane_steps):
        plane_copies.append(send(plane_out.at[plane(*step)], plane_in.at[k], plane_send.at[k],
                                 plane_recv.at[k], plane_id(*step)))
        plane_copies[-1].start()
    final = plane_own[group]
    for k in range(GROUPS - 1):
        plane_copies[k].wait()
        final = final + plane_in[k].astype(F32)

    final = final * (1.0 / total_samples)
    moments = final[0:8]
    ratio = final[8:16] / (moments + DAMPING)
    ring[group] = jnp.concatenate([ratio, moments], axis=0).astype(BF)
    ring_copies = []
    for k, step in enumerate(plane_steps):
        ring_copies.append(send(ring.at[group], ring.at[group], ring_send.at[k],
                                ring_recv.at[k], plane_id(*step)))
        ring_copies[-1].start()
    for c in ring_copies:
        c.wait()

    both = ring[...].astype(F32)
    my_rows = pl.ds(pl.multiple_of(core * 128, 128), 128)
    ratio_full[owner, my_rows, :] = both[:, 0:8, :].reshape(128, LANES).astype(BF)
    moments = both[:, 8:16, :].reshape(128, LANES)
    stats_out[...] = moments.astype(BF)
    last = [send(ratio_full.at[owner, my_rows, :], ratio_full.at[owner, my_rows, :],
                 last_send.at[d - 1], last_recv.at[d - 1], across(d)) for d in (1, 2, 3)]
    for c in last:
        c.start()
    to_twin = [send(ratio_full.at[owner, my_rows, :], ratio_full.at[owner, my_rows, :],
                    last_send.at[3], last_recv.at[3], twin),
               send(stats_out, stats_in, last_send.at[4], last_recv.at[4], twin)]
    for c in to_twin:
        c.start()
    stats_ref[my_rows, :] = stats_out[...].astype(F32)
    for d in (1, 2, 3):
        last[d - 1].wait()
        o = lax.rem(owner + OWNERS - d, OWNERS)
        to_twin.append(send(ratio_full.at[o, my_rows, :], ratio_full.at[o, my_rows, :],
                            last_send.at[4 + d], last_recv.at[4 + d], twin))
        to_twin[-1].start()
    for c in to_twin:
        c.wait()
    twin_rows = pl.ds(pl.multiple_of((1 - core) * 128, 128), 128)
    stats_ref[twin_rows, :] = stats_in[...].astype(F32)

    ratio_all = jnp.concatenate([ratio_full[o] for o in range(OWNERS)], axis=1)
    mixed = lax.dot_general(bo_full[...], ratio_all, (((0,), (0,)), ((), ())),
                            preferred_element_type=F32).astype(BF)
    raw = dot_nt(mixed, bi_full[...])
    for o in range(OWNERS):
        raw_buf[o] = raw[:, o * LANES:(o + 1) * LANES]
    squares = jnp.sum(jnp.sum(raw * raw, axis=0, keepdims=True), axis=1, keepdims=True)
    mean_sq = squares * (1.0 / (channels * 2 * channels))
    update_ref[...] = raw_buf[owner] / jnp.sqrt(mean_sq + 1e-06)


def body(
    block_input_rows, spin_values, conv_weight, conv_bias, readout, energies, basis_out, basis_in
):
    samples, sites, channels = block_input_rows.shape
    vmem = pl.BlockSpec(memory_space=pltpu.VMEM)
    dma = pltpu.SemaphoreType.DMA
    return pl.pallas_call(
        kernel,
        out_shape=(
            jax.ShapeDtypeStruct((channels, LANES), F32),
            jax.ShapeDtypeStruct((channels, LANES), F32),
        ),
        in_specs=[pl.BlockSpec(memory_space=pl.ANY), vmem, vmem, vmem, vmem,
                  pl.BlockSpec(memory_space=pltpu.SMEM), vmem, vmem],
        out_specs=(vmem, vmem),
        scratch_shapes=[
            pltpu.VMEM((samples, sites + DILATION_STEP, channels), BF),
            pltpu.VMEM((channels, sites), BF),
            pltpu.VMEM((samples, channels, 2 * channels), BF),
            pltpu.VMEM((samples, channels, 2 * channels), BF),
            pltpu.VMEM((channels, channels), BF),
            pltpu.VMEM((2 * channels, 2 * channels), BF),
            pltpu.VMEM((channels, LANES), F32),
            pltpu.VMEM((channels, LANES), F32),
            pltpu.VMEM((16, channels), BF),
            pltpu.VMEM((5, 8, LANES), F32),
            pltpu.VMEM((10, 8, LANES), F32),
            pltpu.VMEM((OWNERS, GROUPS, 16, LANES), BF),
            pltpu.VMEM((OWNERS, GROUPS, 16, LANES), BF),
            pltpu.VMEM((OWNERS, GROUPS, 16, LANES), F32),
            pltpu.VMEM((3, GROUPS, 16, LANES), BF),
            pltpu.VMEM((3, GROUPS, 16, LANES), BF),
            pltpu.VMEM((GROUPS, 16, LANES), BF),
            pltpu.VMEM((GROUPS - 1, 16, LANES), BF),
            pltpu.VMEM((GROUPS, 16, LANES), F32),
            pltpu.VMEM((GROUPS, 16, LANES), BF),
            pltpu.VMEM((OWNERS, channels, LANES), BF),
            pltpu.VMEM((channels // 2, LANES), BF),
            pltpu.VMEM((channels // 2, LANES), BF),
            pltpu.VMEM((OWNERS, channels, LANES), F32),
            dma((samples,)),
            dma((6,)), dma((6,)),
            dma((10,)), dma((10,)),
            dma(()), dma(()),
            dma((3,)), dma((3,)),
            dma((GROUPS - 1,)), dma((GROUPS - 1,)),
            dma((GROUPS - 1,)), dma((GROUPS - 1,)),
            dma((8,)), dma((8,)),
        ],
        compiler_params=pltpu.CompilerParams(
            collective_id=0, has_side_effects=True, vmem_limit_bytes=56 << 20),
    )(
        block_input_rows, spin_values, conv_weight,
        conv_bias.reshape(1, channels), readout.reshape(1, channels), energies,
        basis_out.T, basis_in,
    )


def solution(mesh):
    in_specs = (
        P(("walker", "owner"), None, None),
        P(("walker", "owner"), None),
        P(),
        P(),
        P(),
        P(("walker", "owner")),
        P(None, "owner"),
        P(None, "owner"),
    )
    out_specs = (P(None, "owner"), P(None, "owner"))
    return jax.shard_map(body, mesh=mesh, in_specs=in_specs, out_specs=out_specs, check_vma=False)
```

```python
import jax
import jax.numpy as jnp
from jax import lax
from jax.experimental import pallas as pl
from jax.experimental.pallas import tpu as pltpu
from jax.sharding import PartitionSpec as P

DILATION_STEP = 16
DAMPING = 0.01
BF = jnp.bfloat16
F32 = jnp.float32
MESH = pl.DeviceIdType.MESH

GROUPS = 16
OWNERS = 4
LANES = 128


def dot_nt(a, b):
    return lax.dot_general(a, b, (((1,), (1,)), ((), ())), preferred_element_type=F32)


def dot_nn(a, b):
    return jnp.dot(a, b, preferred_element_type=F32)


def wide(value, count):
    return jnp.concatenate([value] * count, axis=1) if count > 1 else value


OFFSETS = sorted(
    [(dx, dy, dz) for dx in range(4) for dy in range(4) for dz in range(4)][1:],
    key=lambda step: -sum(min(d, 4 - d) for d in step),
)


def kernel(
    x_hbm, spin_ref, w_ref, bias_ref, readout_ref, e_ref, bo_ref, bi_ref,
    stats_ref, update_ref,
    xbuf, back_a, back_b, grads, halves, bo_full, bi_full, bias_col, read_col, weight,
    e_out, e_in, core_out, core_in, own, sum_out, sum_in, ring, ring_twin, raw_buf,
    x_sem, basis_send, basis_recv, e_send, e_recv, core_send, core_recv,
    sum_send, sum_recv, ring_send, ring_recv, last_send, last_recv,
):
    samples, sites, channels = x_hbm.shape
    pad = DILATION_STEP
    total_samples = samples * 128
    walker = lax.axis_index("walker")
    owner = lax.axis_index("owner")
    core = lax.rem(walker, 2)
    group = walker // 2
    gx, gz = group // 4, lax.rem(group, 4)
    xs = [gx * 4] + [lax.rem(gx + d, 4) * 4 for d in (1, 2, 3)]
    zs = [gz] + [lax.rem(gz + d, 4) for d in (1, 2, 3)]
    ys = [owner] + [lax.rem(owner + d, 4) for d in (1, 2, 3)]

    def chip(dx, dy, dz):
        return ((xs[dx] + zs[dz]) * 2 + core, ys[dy])

    twin = (group * 2 + (1 - core), owner)
    peers = [twin] + [chip(*s) for s in OFFSETS]

    barrier = pltpu.get_barrier_semaphore()
    for peer in peers:
        pl.semaphore_signal(barrier, inc=1, device_id=peer, device_id_type=MESH)

    def load(i):
        return pltpu.make_async_copy(x_hbm.at[i], xbuf.at[i, pl.ds(pad, sites), :], x_sem.at[i])

    for i in range(samples):
        load(i).start()

    def send(src, dst, ssem, rsem, peer):
        return pltpu.make_async_remote_copy(
            src_ref=src, dst_ref=dst, send_sem=ssem, recv_sem=rsem,
            device_id=peer, device_id_type=MESH,
        )

    bias_col[...] = jnp.broadcast_to(bias_ref[...], (LANES, channels)).T
    read_col[...] = jnp.broadcast_to(readout_ref[...], (LANES, channels)).T
    r = readout_ref[...]
    hi = r.astype(BF).astype(F32)
    mid = (r - hi).astype(BF).astype(F32)
    low = r - hi - mid
    row = lax.broadcasted_iota(jnp.int32, (16, channels), 0)
    spread = jnp.where(row == 0, hi, jnp.where(row == 1, mid, jnp.where(row == 2, low, 0.0)))
    weight[:channels, :] = w_ref[...]
    weight[channels:, :channels] = jnp.zeros((16, channels), BF)
    weight[channels:, channels:] = spread.astype(BF)
    for i in range(samples):
        xbuf[i, 0:pad, :] = jnp.zeros((pad, channels), BF)

    own_rows = pl.ds(pl.multiple_of(owner * 64, 64), 64)
    own_cols = pl.ds(pl.multiple_of(owner * LANES, LANES), LANES)
    bi_half = pl.ds(pl.multiple_of(core * channels, channels), channels)
    bo_full[own_rows, :] = bo_ref[...]
    bi_full[:, own_cols] = bi_ref[...]

    def bo_copies():
        return [send(bo_ref, bo_full.at[own_rows, :], basis_send.at[d - 1],
                     basis_recv.at[d - 1], chip(0, d, 0)) for d in (1, 2, 3)]

    def bi_copies():
        return [send(bi_ref.at[bi_half, :], bi_full.at[bi_half, own_cols], basis_send.at[d + 2],
                     basis_recv.at[d + 2], chip(0, d, 0)) for d in (1, 2, 3)]

    def bi_relays():
        out = []
        for d in (1, 2, 3):
            cols = pl.ds(pl.multiple_of(ys[d] * LANES, LANES), LANES)
            part = bi_full.at[bi_half, cols]
            out.append(send(part, part, basis_send.at[d + 5], basis_recv.at[d + 5], twin))
        return out

    e_sum = e_ref[0]
    for i in range(1, samples):
        e_sum = e_sum + e_ref[i]
    e_out[0] = jnp.full((8, LANES), e_sum, F32)
    stages = [
        [twin],
        [chip(0, d, 0) for d in (1, 2, 3)],
        [chip(k // 4, 0, k % 4) for k in range(1, GROUPS)],
    ]
    first_slot = [0, 1, 4]

    def energy_copies(stage):
        base = first_slot[stage]
        return [send(e_out.at[stage], e_in.at[base + k], e_send.at[base + k],
                     e_recv.at[base + k], peer) for k, peer in enumerate(stages[stage])]

    def energy_start(stage):
        for c in energy_copies(stage):
            c.start()

    def energy_finish(stage):
        copies = energy_copies(stage)
        for c in copies:
            c.wait()
        total = e_out[stage]
        for k in range(len(copies)):
            total = total + e_in[first_slot[stage] + k]
        e_out[stage + 1] = total

    chunk = 256

    def forward(i, back):
        for c in range(sites // chunk):
            lo = c * chunk
            x_prev = xbuf[i, lo:lo + chunk, :]
            x_now = xbuf[i, lo + pad:lo + pad + chunk, :]
            out = dot_nt(weight[...], jnp.concatenate([x_prev, x_now], axis=1))
            act = jnp.tanh(out[:channels] + wide(bias_col[...], chunk // LANES))
            logit = jnp.sum(act * wide(read_col[...], chunk // LANES), axis=0, keepdims=True)
            logit = logit + jnp.sum(out[channels:], axis=0, keepdims=True)
            target = spin_ref[pl.ds(i, 1), lo:lo + chunk].astype(F32)
            signal = 0.5 * (target - jax.nn.sigmoid(logit))
            back[:, lo:lo + chunk] = (signal * (1.0 - act * act)).astype(BF)

    def gradient(i, back):
        scale = wide(read_col[...], channels // LANES)
        b = back[...]
        grads[i, :, :channels] = (dot_nn(b, xbuf[i, :sites, :]) * scale).astype(BF)
        grads[i, :, channels:] = (dot_nn(b, xbuf[i, pad:, :]) * scale).astype(BF)

    @pl.loop(0, samples // 2)
    def _(j):
        @pl.when(j == 1)
        def _():
            pl.semaphore_wait(barrier, len(peers))
            energy_start(0)

        @pl.when(j == 2)
        def _():
            energy_finish(0)
            energy_start(1)
            for c in bo_copies() + bi_copies():
                c.start()

        @pl.when(j == 5)
        def _():
            energy_finish(1)
            energy_start(2)

        @pl.when(j == 7)
        def _():
            for c in bi_copies():
                c.wait()
            for c in bi_relays():
                c.start()

        load(2 * j).wait()
        load(2 * j + 1).wait()
        forward(2 * j, back_a)
        forward(2 * j + 1, back_b)
        gradient(2 * j, back_a)
        gradient(2 * j + 1, back_b)

    for c in bo_copies():
        c.wait()

    @pl.loop(0, samples // 8)
    def _(j):
        for u in range(8):
            halves[8 * j + u] = dot_nn(bo_full[...], grads[8 * j + u]).astype(BF)

    energy_finish(2)
    for c in bi_relays():
        c.wait()

    e_mean = jnp.broadcast_to(e_out[3][0:1, :], (64, LANES)) * (1.0 / total_samples)

    def project(first, tile):
        q, m = tile // 2, tile % 2
        rows = pl.ds(pl.multiple_of(first + q * 64, 64), 64)
        lhs = halves[:, rows, :].reshape(samples * 64, 2 * channels)
        p = dot_nn(lhs, bi_full[:, m * 256:(m + 1) * 256])
        squares = jnp.zeros((64, 256), F32)
        weighted = jnp.zeros((64, 256), F32)
        for n in range(samples):
            pn = p[n * 64:(n + 1) * 64]
            squares = squares + pn * pn
            weighted = weighted + pn * wide(e_ref[n] - e_mean, 2)
        out = []
        for k in range(2):
            cols = slice(k * LANES, (k + 1) * LANES)
            out.append((2 * m + k, q * 8, jnp.concatenate(
                [squares[:, cols].reshape(8, 8, LANES), weighted[:, cols].reshape(8, 8, LANES)],
                axis=1)))
        return out

    for tile in range(4):
        for o, g, block in project((1 - core) * 128, tile):
            core_out[o, g:g + 8] = block.astype(BF)
    core_copy = send(core_out, core_in, core_send, core_recv, twin)
    core_copy.start()
    for tile in range(4):
        for o, g, block in project(core * 128, tile):
            own[o, g:g + 8] = block
    core_copy.wait()

    sum_out[...] = (own[...] + core_in[...].astype(F32)).astype(BF)
    sum_copies = []
    for k, (dx, dy, dz) in enumerate(OFFSETS):
        sum_copies.append(send(sum_out.at[ys[dy], xs[dx] + zs[dz]], sum_in.at[k], sum_send.at[k],
                               sum_recv.at[k], chip(dx, dy, dz)))
        sum_copies[-1].start()
    final = sum_out[owner, group].astype(F32)
    for c in sum_copies:
        c.wait_recv()
    for k in range(len(OFFSETS)):
        final = final + sum_in[k].astype(F32)

    final = final * (1.0 / total_samples)
    moments = final[0:8]
    ratio = final[8:16] / (moments + DAMPING)
    ring[owner, group] = jnp.concatenate([ratio, moments], axis=0).astype(BF)
    tile = ring.at[owner, group]
    ring_copies = {}
    for k, step in enumerate(OFFSETS):
        ring_copies[step] = send(tile, tile, ring_send.at[k], ring_recv.at[k], chip(*step))
        ring_copies[step].start()

    to_twin = []
    for d in (0, 1, 3, 2):
        for step in OFFSETS:
            if step[1] == (4 - d) % 4:
                ring_copies[step].wait_recv()
        to_twin.append(send(ring.at[ys[d]], ring_twin.at[ys[d]], last_send.at[d],
                            last_recv.at[d], twin))
        to_twin[-1].start()

    def back_project(tiles, half):
        both = tiles[...].astype(F32)
        rows = pl.ds(pl.multiple_of(half * 128, 128), 128)
        ratios = jnp.concatenate(
            [both[o, :, 0:8, :].reshape(128, LANES).astype(BF) for o in range(OWNERS)], axis=1)
        stats_ref[rows, :] = tiles[owner].astype(F32)[:, 8:16, :].reshape(128, LANES)
        return lax.dot_general(bo_full[rows, :], ratios, (((0,), (0,)), ((), ())),
                               preferred_element_type=F32)

    mixed = back_project(ring, core)
    for c in to_twin:
        c.wait_recv()
    mixed = (mixed + back_project(ring_twin, 1 - core)).astype(BF)
    raw = dot_nt(mixed, bi_full[...])
    for o in range(OWNERS):
        raw_buf[o] = raw[:, o * LANES:(o + 1) * LANES]
    squares = jnp.sum(jnp.sum(raw * raw, axis=0, keepdims=True), axis=1, keepdims=True)
    mean_sq = squares * (1.0 / (channels * 2 * channels))
    update_ref[...] = raw_buf[owner] / jnp.sqrt(mean_sq + 1e-06)
    for c in sum_copies + list(ring_copies.values()) + to_twin:
        c.wait_send()


def copy_kernel(a_ref, b_ref, a_out, b_out, sems):
    first = pltpu.make_async_copy(a_ref, a_out, sems.at[0])
    second = pltpu.make_async_copy(b_ref, b_out, sems.at[1])
    first.start()
    second.start()
    first.wait()
    second.wait()


def body(
    block_input_rows, spin_values, conv_weight, conv_bias, readout, energies, basis_out, basis_in
):
    samples, sites, channels = block_input_rows.shape
    vmem = pl.BlockSpec(memory_space=pltpu.VMEM)
    dma = pltpu.SemaphoreType.DMA
    result = jax.ShapeDtypeStruct((channels, LANES), F32)
    pairs = pl.pallas_call(
        kernel,
        out_shape=(result, result),
        in_specs=[pl.BlockSpec(memory_space=pl.ANY), vmem, vmem, vmem, vmem,
                  pl.BlockSpec(memory_space=pltpu.SMEM), vmem, vmem],
        out_specs=(vmem, vmem),
        scratch_shapes=[
            pltpu.VMEM((samples, sites + DILATION_STEP, channels), BF),
            pltpu.VMEM((channels, sites), BF),
            pltpu.VMEM((channels, sites), BF),
            pltpu.VMEM((samples, channels, 2 * channels), BF),
            pltpu.VMEM((samples, channels, 2 * channels), BF),
            pltpu.VMEM((channels, channels), BF),
            pltpu.VMEM((2 * channels, 2 * channels), BF),
            pltpu.VMEM((channels, LANES), F32),
            pltpu.VMEM((channels, LANES), F32),
            pltpu.VMEM((channels + 16, 2 * channels), BF),
            pltpu.VMEM((4, 8, LANES), F32),
            pltpu.VMEM((19, 8, LANES), F32),
            pltpu.VMEM((OWNERS, GROUPS, 16, LANES), BF),
            pltpu.VMEM((OWNERS, GROUPS, 16, LANES), BF),
            pltpu.VMEM((OWNERS, GROUPS, 16, LANES), F32),
            pltpu.VMEM((OWNERS, GROUPS, 16, LANES), BF),
            pltpu.VMEM((len(OFFSETS), 16, LANES), BF),
            pltpu.VMEM((OWNERS, GROUPS, 16, LANES), BF),
            pltpu.VMEM((OWNERS, GROUPS, 16, LANES), BF),
            pltpu.VMEM((OWNERS, channels, LANES), F32),
            dma((samples,)),
            dma((9,)), dma((9,)),
            dma((19,)), dma((19,)),
            dma(()), dma(()),
            dma((len(OFFSETS),)), dma((len(OFFSETS),)),
            dma((len(OFFSETS),)), dma((len(OFFSETS),)),
            dma((4,)), dma((4,)),
        ],
        compiler_params=pltpu.CompilerParams(
            collective_id=0, has_side_effects=True, vmem_limit_bytes=56 << 20),
    )(
        block_input_rows, spin_values, conv_weight,
        conv_bias.reshape(1, channels), readout.reshape(1, channels), energies,
        basis_out.T, basis_in,
    )
    anywhere = pl.BlockSpec(memory_space=pl.ANY)
    return pl.pallas_call(
        copy_kernel,
        out_shape=(result, result),
        in_specs=[anywhere, anywhere],
        out_specs=(anywhere, anywhere),
        scratch_shapes=[dma((2,))],
    )(*pairs)


def solution(mesh):
    in_specs = (
        P(("walker", "owner"), None, None),
        P(("walker", "owner"), None),
        P(),
        P(),
        P(),
        P(("walker", "owner")),
        P(None, "owner"),
        P(None, "owner"),
    )
    out_specs = (P(None, "owner"), P(None, "owner"))
    return jax.shard_map(body, mesh=mesh, in_specs=in_specs, out_specs=out_specs, check_vma=False)
```

```python
import jax
import jax.numpy as jnp
from jax import lax
from jax.experimental import pallas as pl
from jax.experimental.pallas import tpu as pltpu
from jax.sharding import PartitionSpec as P

DILATION_STEP = 16
DAMPING = 0.01
BF = jnp.bfloat16
F32 = jnp.float32
MESH = pl.DeviceIdType.MESH

GROUPS = 16
OWNERS = 4
LANES = 128


def dot_nt(a, b):
    return lax.dot_general(a, b, (((1,), (1,)), ((), ())), preferred_element_type=F32)


def dot_nn(a, b):
    return jnp.dot(a, b, preferred_element_type=F32)


def wide(value, count):
    return jnp.concatenate([value] * count, axis=1) if count > 1 else value


OFFSETS = sorted(
    [(dx, dy, dz) for dx in range(4) for dy in range(4) for dz in range(4)][1:],
    key=lambda step: -sum(min(d, 4 - d) for d in step),
)


def kernel(
    x_hbm, spin_hbm, w_hbm, bias_hbm, readout_hbm, e_ref, bo_hbm, bi_hbm,
    stats_ref, update_ref,
    xbuf, spin_ref, bias_ref, readout_ref, back_a, back_b, grads, halves, bo_full, bo_used,
    bo_turned, bi_full, bias_col, read_col, weight,
    e_out, e_in, core_out, core_in, own, sum_out, sum_in, swap_out, swap_in,
    ring, moments_ring, raw_buf,
    x_sem, in_sem, send_sem, recv_sem,
):
    samples, sites, channels = x_hbm.shape
    pad = DILATION_STEP
    total_samples = samples * 128
    walker = lax.axis_index("walker")
    owner = lax.axis_index("owner")
    core = lax.rem(walker, 2)
    group = walker // 2
    gx, gz = group // 4, lax.rem(group, 4)
    xs = [gx * 4] + [lax.rem(gx + d, 4) * 4 for d in (1, 2, 3)]
    zs = [gz] + [lax.rem(gz + d, 4) for d in (1, 2, 3)]
    ys = [owner] + [lax.rem(owner + d, 4) for d in (1, 2, 3)]

    def chip(dx, dy, dz):
        return ((xs[dx] + zs[dz]) * 2 + core, ys[dy])

    twin = (group * 2 + (1 - core), owner)
    across = [((gx * 4 + gz) * 2 + 1 - core, ys[d]) for d in (1, 2, 3)]
    line_x = [chip(d, 0, 0) for d in (1, 2, 3)]
    line_y = [chip(0, d, 0) for d in (1, 2, 3)] + across + [twin]
    line_z = [chip(0, 0, d) for d in (1, 2, 3)]
    peers = line_x + line_z + line_y

    barrier = pltpu.get_barrier_semaphore()
    for peer in peers:
        pl.semaphore_signal(barrier, inc=1, device_id=peer, device_id_type=MESH)

    def load(j):
        pair = pl.ds(2 * j, 2)
        return pltpu.make_async_copy(
            x_hbm.at[pair], xbuf.at[pair, pl.ds(pad, sites), :], x_sem.at[j])

    own_rows = pl.ds(pl.multiple_of(owner * 64, 64), 64)
    own_cols = pl.ds(pl.multiple_of(owner * LANES, LANES), LANES)
    inputs = [
        pltpu.make_async_copy(w_hbm, weight.at[pl.ds(0, channels), :], in_sem.at[0]),
        pltpu.make_async_copy(bias_hbm, bias_ref, in_sem.at[1]),
        pltpu.make_async_copy(readout_hbm, readout_ref, in_sem.at[2]),
        pltpu.make_async_copy(spin_hbm, spin_ref, in_sem.at[3]),
    ]
    bases = [
        pltpu.make_async_copy(bo_hbm, bo_full.at[own_rows, :], in_sem.at[4]),
        pltpu.make_async_copy(bi_hbm, bi_full.at[:, own_cols], in_sem.at[5]),
    ]
    for c in inputs[:3]:
        c.start()
    load(0).start()
    inputs[3].start()
    for j in range(1, samples // 2):
        load(j).start()
    for c in bases:
        c.start()
    for i in range(samples):
        xbuf[i, 0:pad, :] = jnp.zeros((pad, channels), BF)
    for c in inputs:
        c.wait()

    def send(src, dst, ssem, rsem, peer):
        return pltpu.make_async_remote_copy(
            src_ref=src, dst_ref=dst, send_sem=ssem, recv_sem=rsem,
            device_id=peer, device_id_type=MESH,
        )

    bias_col[...] = jnp.broadcast_to(bias_ref[...], (LANES, channels)).T
    read_col[...] = jnp.broadcast_to(readout_ref[...], (LANES, channels)).T
    r = readout_ref[...]
    hi = r.astype(BF).astype(F32)
    mid = (r - hi).astype(BF).astype(F32)
    low = r - hi - mid
    row = lax.broadcasted_iota(jnp.int32, (16, channels), 0)
    spread = jnp.where(row == 0, hi, jnp.where(row == 1, mid, jnp.where(row == 2, low, 0.0)))
    weight[channels:, :channels] = jnp.zeros((16, channels), BF)
    weight[channels:, channels:] = spread.astype(BF)

    bi_half = pl.ds(pl.multiple_of(core * channels, channels), channels)

    def bo_copies():
        part = bo_full.at[own_rows, :]
        return [send(part, part, send_sem.at[0], recv_sem.at[0], chip(0, d, 0))
                for d in (1, 2, 3)]

    def bi_copies():
        part = bi_full.at[bi_half, own_cols]
        return [send(part, part, send_sem.at[1], recv_sem.at[1], chip(0, d, 0))
                for d in (1, 2, 3)]

    def bi_relays():
        out = []
        for d in (1, 2, 3):
            cols = pl.ds(pl.multiple_of(ys[d] * LANES, LANES), LANES)
            part = bi_full.at[bi_half, cols]
            out.append(send(part, part, send_sem.at[2], recv_sem.at[2], twin))
        return out

    bo_all = bo_full.at[pl.ds(0, 192), :]
    bi_all = bi_full.at[pl.ds(0, channels), pl.ds(0, 3 * LANES)]

    def finish(k, part):
        both = send(part, part, send_sem.at[k], recv_sem.at[k], twin)
        both.wait_recv()
        both.wait_send()

    e_sum = e_ref[0]
    for i in range(1, samples):
        e_sum = e_sum + e_ref[i]
    e_out[0] = jnp.full((8, LANES), e_sum, F32)
    stages = [line_y, line_x, line_z]
    first_slot = [0, 7, 10]

    def energy_start(stage):
        for k, peer in enumerate(stages[stage]):
            send(e_out.at[stage], e_in.at[first_slot[stage] + k], send_sem.at[3 + stage],
                 recv_sem.at[3 + stage], peer).start()

    def energy_finish(stage):
        slots = range(first_slot[stage], first_slot[stage] + len(stages[stage]))
        finish(3 + stage, e_in.at[pl.ds(slots[0], len(slots))])
        total = e_out[stage]
        for k in slots:
            total = total + e_in[k]
        e_out[stage + 1] = total

    chunk = 256

    def forward(i, back):
        for c in range(sites // chunk):
            lo = c * chunk
            x_prev = xbuf[i, lo:lo + chunk, :]
            x_now = xbuf[i, lo + pad:lo + pad + chunk, :]
            out = dot_nt(weight[...], jnp.concatenate([x_prev, x_now], axis=1))
            act = jnp.tanh(out[:channels] + wide(bias_col[...], chunk // LANES))
            logit = jnp.sum(act * wide(read_col[...], chunk // LANES), axis=0, keepdims=True)
            logit = logit + jnp.sum(out[channels:], axis=0, keepdims=True)
            target = spin_ref[pl.ds(i, 1), lo:lo + chunk].astype(F32)
            signal = 0.5 * (target - jax.nn.sigmoid(logit))
            back[:, lo:lo + chunk] = (signal * (1.0 - act * act)).astype(BF)

    def gradient(i, back):
        scale = wide(read_col[...], channels // LANES)
        b = back[...]
        grads[i, :, :channels] = (dot_nn(b, xbuf[i, :sites, :]) * scale).astype(BF)
        grads[i, :, channels:] = (dot_nn(b, xbuf[i, pad:, :]) * scale).astype(BF)

    @pl.loop(0, samples // 2)
    def _(j):
        @pl.when(j == 2)
        def _():
            pl.semaphore_wait(barrier, len(peers))
            energy_start(0)
            for c in bases:
                c.wait()
            for c in bo_copies() + bi_copies():
                c.start()

        @pl.when(j == 5)
        def _():
            energy_finish(0)
            energy_start(1)

        load(j).wait()
        forward(2 * j, back_a)
        forward(2 * j + 1, back_b)
        gradient(2 * j, back_a)
        gradient(2 * j + 1, back_b)

    energy_finish(1)
    energy_start(2)
    finish(0, bo_all)
    finish(1, bi_all)
    for c in bi_relays():
        c.start()

    blocks = bo_full[...].astype(F32).reshape(GROUPS, 2, 8, channels)
    bo_used[...] = jnp.concatenate(
        [blocks[:, k].reshape(128, channels) for k in range(2)], axis=0).astype(BF)

    @pl.loop(0, samples // 8)
    def _(j):
        for u in range(8):
            halves[8 * j + u] = dot_nn(bo_used[...], grads[8 * j + u]).astype(BF)

    energy_finish(2)
    finish(2, bi_all)

    e_mean = jnp.broadcast_to(e_out[3][0:1, :], (64, LANES)) * (1.0 / total_samples)

    def project(first, tile):
        q, m = tile // 2, tile % 2
        rows = pl.ds(pl.multiple_of(first + q * 64, 64), 64)
        lhs = halves[:, rows, :].reshape(samples * 64, 2 * channels)
        p = dot_nn(lhs, bi_full[:, m * 256:(m + 1) * 256])
        squares = jnp.zeros((64, 256), F32)
        weighted = jnp.zeros((64, 256), F32)
        for n in range(samples):
            pn = p[n * 64:(n + 1) * 64]
            squares = squares + pn * pn
            weighted = weighted + pn * wide(e_ref[n] - e_mean, 2)
        out = []
        for k in range(2):
            cols = slice(k * LANES, (k + 1) * LANES)
            out.append((2 * m + k, q * 8, jnp.concatenate(
                [squares[:, cols].reshape(8, 8, LANES), weighted[:, cols].reshape(8, 8, LANES)],
                axis=1)))
        return out

    for tile in range(4):
        for o, g, block in project((1 - core) * 128, tile):
            core_out[o, g:g + 8] = block.astype(BF)
    core_copy = send(core_out, core_in, send_sem.at[6], recv_sem.at[6], twin)
    core_copy.start()
    for tile in range(4):
        for o, g, block in project(core * 128, tile):
            own[o, g:g + 8] = block
    core_copy.wait()

    sum_out[...] = (own[...] + core_in[...].astype(F32)).astype(BF)
    for k, (dx, dy, dz) in enumerate(OFFSETS):
        send(sum_out.at[ys[dy], xs[dx] + zs[dz]], sum_in.at[k], send_sem.at[7],
             recv_sem.at[7], chip(dx, dy, dz)).start()
    bo_turned[...] = bo_full[...].T
    final = sum_out[owner, group].astype(F32)
    finish(7, sum_in)
    for k in range(len(OFFSETS)):
        final = final + sum_in[k].astype(F32)

    final = final * (1.0 / total_samples)
    moments = final[0:8]
    ratio = final[8:16] / (moments + DAMPING)
    swap_out[...] = jnp.concatenate([ratio, moments], axis=0)
    swap = send(swap_out, swap_in, send_sem.at[8], recv_sem.at[8], twin)
    swap.start()
    swap.wait()
    mine, other = swap_out[...], swap_in[...]
    upper = jnp.where(core == 0, mine, other)
    lower = jnp.where(core == 0, other, mine)
    ring[owner, group] = jnp.concatenate([upper[0:8], lower[0:8]], axis=0).astype(BF)
    moments_ring[group] = jnp.concatenate([upper[8:16], lower[8:16]], axis=0).astype(BF)
    tile = ring.at[owner, group]
    for dx, dy, dz in OFFSETS:
        send(tile, tile, send_sem.at[9], recv_sem.at[9], chip(dx, dy, dz)).start()
    tile = moments_ring.at[group]
    for dx, dy, dz in OFFSETS:
        if dy == 0:
            send(tile, tile, send_sem.at[10], recv_sem.at[10], chip(dx, dy, dz)).start()
    ring_all = send(sum_in, sum_in, send_sem.at[9], recv_sem.at[9], twin)
    stat_all = moments_ring.at[pl.ds(0, GROUPS - 1)]
    stat_all = send(stat_all, stat_all, send_sem.at[10], recv_sem.at[10], twin)
    ring_all.wait_recv()

    ratios = jnp.concatenate(
        [ring[o].reshape(channels, LANES) for o in range(OWNERS)], axis=1)
    mixed = dot_nn(bo_turned[...], ratios).astype(BF)
    raw = dot_nt(mixed, bi_full[...])
    for o in range(OWNERS):
        raw_buf[o] = raw[:, o * LANES:(o + 1) * LANES]
    squares = jnp.sum(jnp.sum(raw * raw, axis=0, keepdims=True), axis=1, keepdims=True)
    mean_sq = squares * (1.0 / (channels * 2 * channels))
    update_ref[...] = raw_buf[owner] / jnp.sqrt(mean_sq + 1e-06)
    stat_all.wait_recv()
    stats_ref[...] = moments_ring[...].reshape(channels, LANES).astype(F32)
    ring_all.wait_send()
    stat_all.wait_send()


def copy_kernel(a_ref, b_ref, a_out, b_out):
    a_out[...] = a_ref[...]
    b_out[...] = b_ref[...]


def body(
    block_input_rows, spin_values, conv_weight, conv_bias, readout, energies, basis_out, basis_in
):
    samples, sites, channels = block_input_rows.shape
    vmem = pl.BlockSpec(memory_space=pltpu.VMEM)
    anywhere = pl.BlockSpec(memory_space=pl.ANY)
    dma = pltpu.SemaphoreType.DMA
    result = jax.ShapeDtypeStruct((channels, LANES), F32)
    pairs = pl.pallas_call(
        kernel,
        out_shape=(result, result),
        in_specs=[anywhere] * 5 + [pl.BlockSpec(memory_space=pltpu.SMEM)] + [anywhere] * 2,
        out_specs=(vmem, vmem),
        scratch_shapes=[
            pltpu.VMEM((samples, sites + DILATION_STEP, channels), BF),
            pltpu.VMEM((samples, sites), jnp.int32),
            pltpu.VMEM((1, channels), F32),
            pltpu.VMEM((1, channels), F32),
            pltpu.VMEM((channels, sites), BF),
            pltpu.VMEM((channels, sites), BF),
            pltpu.VMEM((samples, channels, 2 * channels), BF),
            pltpu.VMEM((samples, channels, 2 * channels), BF),
            pltpu.VMEM((channels, channels), BF),
            pltpu.VMEM((channels, channels), BF),
            pltpu.VMEM((channels, channels), BF),
            pltpu.VMEM((2 * channels, 2 * channels), BF),
            pltpu.VMEM((channels, LANES), F32),
            pltpu.VMEM((channels, LANES), F32),
            pltpu.VMEM((channels + 16, 2 * channels), BF),
            pltpu.VMEM((4, 8, LANES), F32),
            pltpu.VMEM((13, 8, LANES), F32),
            pltpu.VMEM((OWNERS, GROUPS, 16, LANES), BF),
            pltpu.VMEM((OWNERS, GROUPS, 16, LANES), BF),
            pltpu.VMEM((OWNERS, GROUPS, 16, LANES), F32),
            pltpu.VMEM((OWNERS, GROUPS, 16, LANES), BF),
            pltpu.VMEM((len(OFFSETS), 16, LANES), BF),
            pltpu.VMEM((16, LANES), F32),
            pltpu.VMEM((16, LANES), F32),
            pltpu.VMEM((OWNERS, GROUPS, 16, LANES), BF),
            pltpu.VMEM((GROUPS, 16, LANES), BF),
            pltpu.VMEM((OWNERS, channels, LANES), F32),
            dma((samples // 2,)), dma((6,)), dma((11,)), dma((11,)),
        ],
        compiler_params=pltpu.CompilerParams(
            collective_id=0, has_side_effects=True, vmem_limit_bytes=56 << 20),
    )(
        block_input_rows, spin_values, conv_weight,
        conv_bias.reshape(1, channels), readout.reshape(1, channels), energies,
        basis_out.T, basis_in,
    )
    return pl.pallas_call(
        copy_kernel,
        out_shape=(result, result),
        in_specs=[vmem, vmem],
        out_specs=(vmem, vmem),
    )(*pairs)


def solution(mesh):
    in_specs = (
        P(("walker", "owner"), None, None),
        P(("walker", "owner"), None),
        P(),
        P(),
        P(),
        P(("walker", "owner")),
        P(None, "owner"),
        P(None, "owner"),
    )
    out_specs = (P(None, "owner"), P(None, "owner"))
    return jax.shard_map(body, mesh=mesh, in_specs=in_specs, out_specs=out_specs, check_vma=False)
```

```python
import jax
import jax.numpy as jnp
from jax import lax
from jax.experimental import pallas as pl
from jax.experimental.pallas import tpu as pltpu
from jax.sharding import PartitionSpec as P

DILATION_STEP = 16
DAMPING = 0.01
BF = jnp.bfloat16
F32 = jnp.float32
MESH = pl.DeviceIdType.MESH

GROUPS = 16
OWNERS = 4
LANES = 128


def dot_nt(a, b):
    return lax.dot_general(a, b, (((1,), (1,)), ((), ())), preferred_element_type=F32)


def dot_nn(a, b):
    return jnp.dot(a, b, preferred_element_type=F32)


def wide(value, count):
    return jnp.concatenate([value] * count, axis=1) if count > 1 else value


OFFSETS = sorted(
    [(dx, dy, dz) for dx in range(4) for dy in range(4) for dz in range(4)][1:],
    key=lambda step: -sum(min(d, 4 - d) for d in step),
)


def kernel(
    x_hbm, spin_hbm, w_hbm, bias_hbm, readout_hbm, e_ref, bo_hbm, bi_hbm,
    stats_ref, update_ref,
    xbuf, spin_ref, bias_ref, readout_ref, back_a, back_b, grads, halves, bo_full, bo_used,
    bo_turned, bi_full, bias_col, read_col, weight,
    e_out, e_in, core_out, core_in, own, sum_out, sum_in, swap_out, swap_in,
    ring, moments_ring, raw_buf,
    x_sem, in_sem, send_sem, recv_sem,
):
    samples, sites, channels = x_hbm.shape
    pad = DILATION_STEP
    total_samples = samples * 128
    walker = lax.axis_index("walker")
    owner = lax.axis_index("owner")
    core = lax.rem(walker, 2)
    group = walker // 2
    gx, gz = group // 4, lax.rem(group, 4)
    xs = [gx * 4] + [lax.rem(gx + d, 4) * 4 for d in (1, 2, 3)]
    zs = [gz] + [lax.rem(gz + d, 4) for d in (1, 2, 3)]
    ys = [owner] + [lax.rem(owner + d, 4) for d in (1, 2, 3)]

    def chip(dx, dy, dz):
        return ((xs[dx] + zs[dz]) * 2 + core, ys[dy])

    twin = (group * 2 + (1 - core), owner)
    across = [((gx * 4 + gz) * 2 + 1 - core, ys[d]) for d in (1, 2, 3)]
    line_x = [chip(d, 0, 0) for d in (1, 2, 3)]
    line_y = [chip(0, d, 0) for d in (1, 2, 3)] + across + [twin]
    line_z = [chip(0, 0, d) for d in (1, 2, 3)]
    peers = line_x + line_z + line_y

    barrier = pltpu.get_barrier_semaphore()
    for peer in peers:
        pl.semaphore_signal(barrier, inc=1, device_id=peer, device_id_type=MESH)

    def load(j):
        pair = pl.ds(2 * j, 2)
        return pltpu.make_async_copy(
            x_hbm.at[pair], xbuf.at[pair, pl.ds(pad, sites), :], x_sem.at[j])

    own_rows = pl.ds(pl.multiple_of(owner * 64, 64), 64)
    own_cols = pl.ds(pl.multiple_of(owner * LANES, LANES), LANES)
    inputs = [
        pltpu.make_async_copy(w_hbm, weight.at[pl.ds(0, channels), :], in_sem.at[0]),
        pltpu.make_async_copy(bias_hbm, bias_ref, in_sem.at[1]),
        pltpu.make_async_copy(readout_hbm, readout_ref, in_sem.at[2]),
        pltpu.make_async_copy(spin_hbm, spin_ref, in_sem.at[3]),
    ]
    bases = [
        pltpu.make_async_copy(bo_hbm, bo_full.at[own_rows, :], in_sem.at[4]),
        pltpu.make_async_copy(bi_hbm, bi_full.at[:, own_cols], in_sem.at[5]),
    ]
    load(0).start()
    for c in inputs:
        c.start()
    for i in range(samples):
        xbuf[i, 0:pad, :] = jnp.zeros((pad, channels), BF)
    for c in inputs:
        c.wait()
    for j in range(1, samples // 2):
        load(j).start()
    for c in bases:
        c.start()

    def send(src, dst, ssem, rsem, peer):
        return pltpu.make_async_remote_copy(
            src_ref=src, dst_ref=dst, send_sem=ssem, recv_sem=rsem,
            device_id=peer, device_id_type=MESH,
        )

    bias_col[...] = jnp.broadcast_to(bias_ref[...], (LANES, channels)).T
    read_col[...] = jnp.broadcast_to(readout_ref[...], (LANES, channels)).T
    r = readout_ref[...]
    hi = r.astype(BF).astype(F32)
    mid = (r - hi).astype(BF).astype(F32)
    low = r - hi - mid
    row = lax.broadcasted_iota(jnp.int32, (16, channels), 0)
    spread = jnp.where(row == 0, hi, jnp.where(row == 1, mid, jnp.where(row == 2, low, 0.0)))
    weight[channels:, :channels] = jnp.zeros((16, channels), BF)
    weight[channels:, channels:] = spread.astype(BF)

    bi_half = pl.ds(pl.multiple_of(core * channels, channels), channels)

    def bo_copies():
        part = bo_full.at[own_rows, :]
        return [send(part, part, send_sem.at[0], recv_sem.at[0], chip(0, d, 0))
                for d in (1, 2, 3)]

    def bi_copies():
        part = bi_full.at[bi_half, own_cols]
        return [send(part, part, send_sem.at[1], recv_sem.at[1], chip(0, d, 0))
                for d in (1, 2, 3)]

    def bi_relays():
        out = []
        for d in (1, 2, 3):
            cols = pl.ds(pl.multiple_of(ys[d] * LANES, LANES), LANES)
            part = bi_full.at[bi_half, cols]
            out.append(send(part, part, send_sem.at[2], recv_sem.at[2], twin))
        return out

    bo_all = bo_full.at[pl.ds(0, 192), :]
    bi_all = bi_full.at[pl.ds(0, channels), pl.ds(0, 3 * LANES)]

    def finish(k, part):
        both = send(part, part, send_sem.at[k], recv_sem.at[k], twin)
        both.wait_recv()
        both.wait_send()

    e_sum = e_ref[0]
    for i in range(1, samples):
        e_sum = e_sum + e_ref[i]
    e_out[0] = jnp.full((8, LANES), e_sum, F32)
    stages = [line_y, line_x, line_z]
    first_slot = [0, 7, 10]

    def energy_start(stage):
        for k, peer in enumerate(stages[stage]):
            send(e_out.at[stage], e_in.at[first_slot[stage] + k], send_sem.at[3 + stage],
                 recv_sem.at[3 + stage], peer).start()

    def energy_finish(stage):
        slots = range(first_slot[stage], first_slot[stage] + len(stages[stage]))
        finish(3 + stage, e_in.at[pl.ds(slots[0], len(slots))])
        total = e_out[stage]
        for k in slots:
            total = total + e_in[k]
        e_out[stage + 1] = total

    chunk = 256

    def forward(i, back):
        for c in range(sites // chunk):
            lo = c * chunk
            x_prev = xbuf[i, lo:lo + chunk, :]
            x_now = xbuf[i, lo + pad:lo + pad + chunk, :]
            out = dot_nt(weight[...], jnp.concatenate([x_prev, x_now], axis=1))
            act = jnp.tanh(out[:channels] + wide(bias_col[...], chunk // LANES))
            logit = jnp.sum(act * wide(read_col[...], chunk // LANES), axis=0, keepdims=True)
            logit = logit + jnp.sum(out[channels:], axis=0, keepdims=True)
            target = spin_ref[pl.ds(i, 1), lo:lo + chunk].astype(F32)
            signal = 0.5 * (target - jax.nn.sigmoid(logit))
            back[:, lo:lo + chunk] = (signal * (1.0 - act * act)).astype(BF)

    def gradient(i, back):
        scale = wide(read_col[...], channels // LANES)
        b = back[...]
        grads[i, :, :channels] = (dot_nn(b, xbuf[i, :sites, :]) * scale).astype(BF)
        grads[i, :, channels:] = (dot_nn(b, xbuf[i, pad:, :]) * scale).astype(BF)

    @pl.loop(0, samples // 2)
    def _(j):
        @pl.when(j == 2)
        def _():
            pl.semaphore_wait(barrier, len(peers))
            energy_start(0)
            for c in bases:
                c.wait()
            for c in bo_copies() + bi_copies():
                c.start()

        @pl.when(j == 4)
        def _():
            energy_finish(0)
            energy_start(1)

        @pl.when(j == 6)
        def _():
            energy_finish(1)
            energy_start(2)

        @pl.when(j == 7)
        def _():
            finish(1, bi_all)
            for c in bi_relays():
                c.start()

        load(j).wait()
        forward(2 * j, back_a)
        forward(2 * j + 1, back_b)
        gradient(2 * j, back_a)
        gradient(2 * j + 1, back_b)

    finish(0, bo_all)

    blocks = bo_full[...].astype(F32).reshape(GROUPS, 2, 8, channels)
    bo_used[...] = jnp.concatenate(
        [blocks[:, k].reshape(128, channels) for k in range(2)], axis=0).astype(BF)

    @pl.loop(0, samples // 8)
    def _(j):
        for u in range(8):
            halves[8 * j + u] = dot_nn(bo_used[...], grads[8 * j + u]).astype(BF)

    energy_finish(2)
    finish(2, bi_all)

    e_mean = jnp.broadcast_to(e_out[3][0:1, :], (64, LANES)) * (1.0 / total_samples)

    def project(first, tile):
        q, m = tile // 2, tile % 2
        rows = pl.ds(pl.multiple_of(first + q * 64, 64), 64)
        lhs = halves[:, rows, :].reshape(samples * 64, 2 * channels)
        p = dot_nn(lhs, bi_full[:, m * 256:(m + 1) * 256])
        squares = jnp.zeros((64, 256), F32)
        weighted = jnp.zeros((64, 256), F32)
        for n in range(samples):
            pn = p[n * 64:(n + 1) * 64]
            squares = squares + pn * pn
            weighted = weighted + pn * wide(e_ref[n] - e_mean, 2)
        out = []
        for k in range(2):
            cols = slice(k * LANES, (k + 1) * LANES)
            out.append((2 * m + k, q * 8, jnp.concatenate(
                [squares[:, cols].reshape(8, 8, LANES), weighted[:, cols].reshape(8, 8, LANES)],
                axis=1)))
        return out

    for tile in range(4):
        for o, g, block in project((1 - core) * 128, tile):
            core_out[o, g:g + 8] = block.astype(BF)
    core_copy = send(core_out, core_in, send_sem.at[6], recv_sem.at[6], twin)
    core_copy.start()
    for tile in range(4):
        for o, g, block in project(core * 128, tile):
            own[o, g:g + 8] = block
    core_copy.wait()

    sum_out[...] = (own[...] + core_in[...].astype(F32)).astype(BF)
    for k, (dx, dy, dz) in enumerate(OFFSETS):
        send(sum_out.at[ys[dy], xs[dx] + zs[dz]], sum_in.at[k], send_sem.at[7],
             recv_sem.at[7], chip(dx, dy, dz)).start()
    bo_turned[...] = bo_full[...].T
    final = sum_out[owner, group].astype(F32)
    finish(7, sum_in)
    for k in range(len(OFFSETS)):
        final = final + sum_in[k].astype(F32)

    final = final * (1.0 / total_samples)
    moments = final[0:8]
    ratio = final[8:16] / (moments + DAMPING)
    swap_out[...] = jnp.concatenate([ratio, moments], axis=0)
    swap = send(swap_out, swap_in, send_sem.at[8], recv_sem.at[8], twin)
    swap.start()
    swap.wait()
    mine, other = swap_out[...], swap_in[...]
    upper = jnp.where(core == 0, mine, other)
    lower = jnp.where(core == 0, other, mine)
    ring[owner, group] = jnp.concatenate([upper[0:8], lower[0:8]], axis=0).astype(BF)
    moments_ring[group] = jnp.concatenate([upper[8:16], lower[8:16]], axis=0).astype(BF)
    tile = ring.at[owner, group]
    for dx, dy, dz in OFFSETS:
        send(tile, tile, send_sem.at[9], recv_sem.at[9], chip(dx, dy, dz)).start()
    tile = moments_ring.at[group]
    for dx, dy, dz in OFFSETS:
        if dy == 0:
            send(tile, tile, send_sem.at[10], recv_sem.at[10], chip(dx, dy, dz)).start()
    ring_all = send(sum_in, sum_in, send_sem.at[9], recv_sem.at[9], twin)
    stat_all = moments_ring.at[pl.ds(0, GROUPS - 1)]
    stat_all = send(stat_all, stat_all, send_sem.at[10], recv_sem.at[10], twin)
    ring_all.wait_recv()

    ratios = jnp.concatenate(
        [ring[o].reshape(channels, LANES) for o in range(OWNERS)], axis=1)
    mixed = dot_nn(bo_turned[...], ratios).astype(BF)
    raw = dot_nt(mixed, bi_full[...])
    for o in range(OWNERS):
        raw_buf[o] = raw[:, o * LANES:(o + 1) * LANES]
    squares = jnp.sum(jnp.sum(raw * raw, axis=0, keepdims=True), axis=1, keepdims=True)
    mean_sq = squares * (1.0 / (channels * 2 * channels))
    update_ref[...] = raw_buf[owner] / jnp.sqrt(mean_sq + 1e-06)
    stat_all.wait_recv()
    stats_ref[...] = moments_ring[...].reshape(channels, LANES).astype(F32)
    ring_all.wait_send()
    stat_all.wait_send()


def copy_kernel(a_ref, b_ref, a_out, b_out):
    a_out[...] = a_ref[...]
    b_out[...] = b_ref[...]


def body(
    block_input_rows, spin_values, conv_weight, conv_bias, readout, energies, basis_out, basis_in
):
    samples, sites, channels = block_input_rows.shape
    vmem = pl.BlockSpec(memory_space=pltpu.VMEM)
    anywhere = pl.BlockSpec(memory_space=pl.ANY)
    dma = pltpu.SemaphoreType.DMA
    result = jax.ShapeDtypeStruct((channels, LANES), F32)
    pairs = pl.pallas_call(
        kernel,
        out_shape=(result, result),
        in_specs=[anywhere] * 5 + [pl.BlockSpec(memory_space=pltpu.SMEM)] + [anywhere] * 2,
        out_specs=(vmem, vmem),
        scratch_shapes=[
            pltpu.VMEM((samples, sites + DILATION_STEP, channels), BF),
            pltpu.VMEM((samples, sites), jnp.int32),
            pltpu.VMEM((1, channels), F32),
            pltpu.VMEM((1, channels), F32),
            pltpu.VMEM((channels, sites), BF),
            pltpu.VMEM((channels, sites), BF),
            pltpu.VMEM((samples, channels, 2 * channels), BF),
            pltpu.VMEM((samples, channels, 2 * channels), BF),
            pltpu.VMEM((channels, channels), BF),
            pltpu.VMEM((channels, channels), BF),
            pltpu.VMEM((channels, channels), BF),
            pltpu.VMEM((2 * channels, 2 * channels), BF),
            pltpu.VMEM((channels, LANES), F32),
            pltpu.VMEM((channels, LANES), F32),
            pltpu.VMEM((channels + 16, 2 * channels), BF),
            pltpu.VMEM((4, 8, LANES), F32),
            pltpu.VMEM((13, 8, LANES), F32),
            pltpu.VMEM((OWNERS, GROUPS, 16, LANES), BF),
            pltpu.VMEM((OWNERS, GROUPS, 16, LANES), BF),
            pltpu.VMEM((OWNERS, GROUPS, 16, LANES), F32),
            pltpu.VMEM((OWNERS, GROUPS, 16, LANES), BF),
            pltpu.VMEM((len(OFFSETS), 16, LANES), BF),
            pltpu.VMEM((16, LANES), F32),
            pltpu.VMEM((16, LANES), F32),
            pltpu.VMEM((OWNERS, GROUPS, 16, LANES), BF),
            pltpu.VMEM((GROUPS, 16, LANES), BF),
            pltpu.VMEM((OWNERS, channels, LANES), F32),
            dma((samples // 2,)), dma((6,)), dma((11,)), dma((11,)),
        ],
        compiler_params=pltpu.CompilerParams(
            collective_id=0, has_side_effects=True, vmem_limit_bytes=56 << 20),
    )(
        block_input_rows, spin_values, conv_weight,
        conv_bias.reshape(1, channels), readout.reshape(1, channels), energies,
        basis_out.T, basis_in,
    )
    return pl.pallas_call(
        copy_kernel,
        out_shape=(result, result),
        in_specs=[vmem, vmem],
        out_specs=(vmem, vmem),
    )(*pairs)


def solution(mesh):
    in_specs = (
        P(("walker", "owner"), None, None),
        P(("walker", "owner"), None),
        P(),
        P(),
        P(),
        P(("walker", "owner")),
        P(None, "owner"),
        P(None, "owner"),
    )
    out_specs = (P(None, "owner"), P(None, "owner"))
    return jax.shard_map(body, mesh=mesh, in_specs=in_specs, out_specs=out_specs, check_vma=False)
```

```python
import jax
import jax.numpy as jnp
from jax import lax
from jax.experimental import pallas as pl
from jax.experimental.pallas import tpu as pltpu
from jax.sharding import PartitionSpec as P

DILATION_STEP = 16
DAMPING = 0.01
BF = jnp.bfloat16
F32 = jnp.float32
MESH = pl.DeviceIdType.MESH

GROUPS = 16
OWNERS = 4
LANES = 128


def dot_nt(a, b):
    return lax.dot_general(a, b, (((1,), (1,)), ((), ())), preferred_element_type=F32)


def dot_nn(a, b):
    return jnp.dot(a, b, preferred_element_type=F32)


def wide(value, count):
    return jnp.concatenate([value] * count, axis=1) if count > 1 else value


OFFSETS = sorted(
    [(dx, dy, dz) for dx in range(4) for dy in range(4) for dz in range(4)][1:],
    key=lambda step: -sum(min(d, 4 - d) for d in step),
)


def kernel(
    x_hbm, spin_hbm, w_hbm, bias_hbm, readout_hbm, e_ref, bo_hbm, bi_hbm,
    stats_ref, update_ref,
    xbuf, spin_ref, bias_ref, readout_ref, back_a, back_b, grads, halves, bo_full, bo_used,
    bo_turned, bi_full, bias_col, read_col, weight,
    e_out, e_in, core_out, core_in, own, plain_out, plain_in, own_plain, sum_out, sum_in, swap_out, swap_in,
    ring, moments_ring, raw_buf,
    x_sem, in_sem, send_sem, recv_sem,
):
    samples, sites, channels = x_hbm.shape
    pad = DILATION_STEP
    total_samples = samples * 128
    walker = lax.axis_index("walker")
    owner = lax.axis_index("owner")
    core = lax.rem(walker, 2)
    group = walker // 2
    gx, gz = group // 4, lax.rem(group, 4)
    xs = [gx * 4] + [lax.rem(gx + d, 4) * 4 for d in (1, 2, 3)]
    zs = [gz] + [lax.rem(gz + d, 4) for d in (1, 2, 3)]
    ys = [owner] + [lax.rem(owner + d, 4) for d in (1, 2, 3)]

    def chip(dx, dy, dz):
        return ((xs[dx] + zs[dz]) * 2 + core, ys[dy])

    twin = (group * 2 + (1 - core), owner)
    across = [((gx * 4 + gz) * 2 + 1 - core, ys[d]) for d in (1, 2, 3)]
    line_x = [chip(d, 0, 0) for d in (1, 2, 3)]
    line_y = [chip(0, d, 0) for d in (1, 2, 3)] + across + [twin]
    line_z = [chip(0, 0, d) for d in (1, 2, 3)]
    peers = line_x + line_z + line_y

    barrier = pltpu.get_barrier_semaphore()
    for peer in peers:
        pl.semaphore_signal(barrier, inc=1, device_id=peer, device_id_type=MESH)

    def load(j):
        pair = pl.ds(2 * j, 2)
        return pltpu.make_async_copy(
            x_hbm.at[pair], xbuf.at[pair, pl.ds(pad, sites), :], x_sem.at[j])

    own_rows = pl.ds(pl.multiple_of(owner * 64, 64), 64)
    own_cols = pl.ds(pl.multiple_of(owner * LANES, LANES), LANES)
    inputs = [
        pltpu.make_async_copy(w_hbm, weight.at[pl.ds(0, channels), :], in_sem.at[0]),
        pltpu.make_async_copy(bias_hbm, bias_ref, in_sem.at[1]),
        pltpu.make_async_copy(readout_hbm, readout_ref, in_sem.at[2]),
        pltpu.make_async_copy(spin_hbm, spin_ref, in_sem.at[3]),
    ]
    bases = [
        pltpu.make_async_copy(bo_hbm, bo_full.at[own_rows, :], in_sem.at[4]),
        pltpu.make_async_copy(bi_hbm, bi_full.at[:, own_cols], in_sem.at[5]),
    ]
    load(0).start()
    for c in inputs:
        c.start()
    for i in range(samples):
        xbuf[i, 0:pad, :] = jnp.zeros((pad, channels), BF)
    for c in inputs:
        c.wait()
    for j in range(1, samples // 2):
        load(j).start()
    for c in bases:
        c.start()

    def send(src, dst, ssem, rsem, peer):
        return pltpu.make_async_remote_copy(
            src_ref=src, dst_ref=dst, send_sem=ssem, recv_sem=rsem,
            device_id=peer, device_id_type=MESH,
        )

    bias_col[...] = jnp.broadcast_to(bias_ref[...], (LANES, channels)).T
    read_col[...] = jnp.broadcast_to(readout_ref[...], (LANES, channels)).T
    r = readout_ref[...]
    hi = r.astype(BF).astype(F32)
    mid = (r - hi).astype(BF).astype(F32)
    low = r - hi - mid
    row = lax.broadcasted_iota(jnp.int32, (16, channels), 0)
    spread = jnp.where(row == 0, hi, jnp.where(row == 1, mid, jnp.where(row == 2, low, 0.0)))
    weight[channels:, :channels] = jnp.zeros((16, channels), BF)
    weight[channels:, channels:] = spread.astype(BF)

    bi_half = pl.ds(pl.multiple_of(core * channels, channels), channels)

    def bo_copies():
        part = bo_full.at[own_rows, :]
        return [send(part, part, send_sem.at[0], recv_sem.at[0], chip(0, d, 0))
                for d in (1, 2, 3)]

    def bi_copies():
        part = bi_full.at[bi_half, own_cols]
        return [send(part, part, send_sem.at[1], recv_sem.at[1], chip(0, d, 0))
                for d in (1, 2, 3)]

    def bi_relays():
        out = []
        for d in (1, 2, 3):
            cols = pl.ds(pl.multiple_of(ys[d] * LANES, LANES), LANES)
            part = bi_full.at[bi_half, cols]
            out.append(send(part, part, send_sem.at[2], recv_sem.at[2], twin))
        return out

    bo_all = bo_full.at[pl.ds(0, 192), :]
    bi_all = bi_full.at[pl.ds(0, channels), pl.ds(0, 3 * LANES)]

    def finish(k, part):
        both = send(part, part, send_sem.at[k], recv_sem.at[k], twin)
        both.wait_recv()
        both.wait_send()

    e_sum = e_ref[0]
    for i in range(1, samples):
        e_sum = e_sum + e_ref[i]
    e_out[0] = jnp.full((8, LANES), e_sum, F32)
    stages = [line_y, line_x, line_z]
    first_slot = [0, 7, 10]

    def energy_start(stage):
        for k, peer in enumerate(stages[stage]):
            send(e_out.at[stage], e_in.at[first_slot[stage] + k], send_sem.at[3 + stage],
                 recv_sem.at[3 + stage], peer).start()

    def energy_finish(stage):
        slots = range(first_slot[stage], first_slot[stage] + len(stages[stage]))
        finish(3 + stage, e_in.at[pl.ds(slots[0], len(slots))])
        total = e_out[stage]
        for k in slots:
            total = total + e_in[k]
        e_out[stage + 1] = total

    chunk = 256

    def forward(i, back):
        for c in range(sites // chunk):
            lo = c * chunk
            x_prev = xbuf[i, lo:lo + chunk, :]
            x_now = xbuf[i, lo + pad:lo + pad + chunk, :]
            out = dot_nt(weight[...], jnp.concatenate([x_prev, x_now], axis=1))
            act = jnp.tanh(out[:channels] + wide(bias_col[...], chunk // LANES))
            logit = jnp.sum(act * wide(read_col[...], chunk // LANES), axis=0, keepdims=True)
            logit = logit + jnp.sum(out[channels:], axis=0, keepdims=True)
            target = spin_ref[pl.ds(i, 1), lo:lo + chunk].astype(F32)
            signal = 0.5 * (target - jax.nn.sigmoid(logit))
            back[:, lo:lo + chunk] = (signal * (1.0 - act * act)).astype(BF)

    def gradient(i, back):
        scale = wide(read_col[...], channels // LANES)
        b = back[...]
        grads[i, :, :channels] = (dot_nn(b, xbuf[i, :sites, :]) * scale).astype(BF)
        grads[i, :, channels:] = (dot_nn(b, xbuf[i, pad:, :]) * scale).astype(BF)

    @pl.loop(0, samples // 2)
    def _(j):
        @pl.when(j == 2)
        def _():
            pl.semaphore_wait(barrier, len(peers))
            energy_start(0)
            for c in bases:
                c.wait()
            for c in bo_copies() + bi_copies():
                c.start()

        @pl.when(j == 5)
        def _():
            energy_finish(0)
            energy_start(1)

        load(j).wait()
        forward(2 * j, back_a)
        forward(2 * j + 1, back_b)
        gradient(2 * j, back_a)
        gradient(2 * j + 1, back_b)

    energy_finish(1)
    energy_start(2)
    finish(0, bo_all)
    finish(1, bi_all)
    for c in bi_relays():
        c.start()

    blocks = bo_full[...].astype(F32).reshape(GROUPS, 2, 8, channels)
    bo_used[...] = jnp.concatenate(
        [blocks[:, k].reshape(128, channels) for k in range(2)], axis=0).astype(BF)

    @pl.loop(0, samples // 8)
    def _(j):
        for u in range(8):
            halves[8 * j + u] = dot_nn(bo_used[...], grads[8 * j + u]).astype(BF)

    finish(2, bi_all)

    e_local = e_sum * (1.0 / samples)

    def project(first, tile):
        q, m = tile // 2, tile % 2
        rows = pl.ds(pl.multiple_of(first + q * 64, 64), 64)
        lhs = halves[:, rows, :].reshape(samples * 64, 2 * channels)
        p = dot_nn(lhs, bi_full[:, m * 256:(m + 1) * 256])
        squares = jnp.zeros((64, 256), F32)
        weighted = jnp.zeros((64, 256), F32)
        plain = jnp.zeros((64, 256), F32)
        for n in range(samples):
            pn = p[n * 64:(n + 1) * 64]
            squares = squares + pn * pn
            weighted = weighted + pn * (e_ref[n] - e_local)
            plain = plain + pn
        out = []
        for k in range(2):
            cols = slice(k * LANES, (k + 1) * LANES)
            parts = [v[:, cols].reshape(8, 8, LANES) for v in (squares, weighted)]
            out.append((2 * m + k, q, jnp.concatenate(parts, axis=1), plain[:, cols]))
        return out

    for tile in range(4):
        for o, q, block, plain in project((1 - core) * 128, tile):
            core_out[o, q * 8:q * 8 + 8] = block.astype(BF)
            plain_out[o, q * 64:q * 64 + 64] = plain.astype(BF)
    core_copy = send(core_out, core_in, send_sem.at[6], recv_sem.at[6], twin)
    core_copy.start()
    plain_copy = send(plain_out, plain_in, send_sem.at[11], recv_sem.at[11], twin)
    plain_copy.start()
    for tile in range(4):
        for o, q, block, plain in project(core * 128, tile):
            own[o, q * 8:q * 8 + 8] = block
            own_plain[o, q * 64:q * 64 + 64] = plain
    energy_finish(2)
    e_mean = e_out[3][0:1, :] * (1.0 / total_samples)
    here = e_out[0][0:1, :] * (1.0 / samples) - e_mean
    there = e_in[6][0:1, :] * (1.0 / samples) - e_mean
    core_copy.wait()
    plain_copy.wait()

    for o in range(OWNERS):
        both = own[o] + core_in[o].astype(F32)
        shift = own_plain[o] * here + plain_in[o].astype(F32) * there
        sum_out[o] = jnp.concatenate(
            [both[:, :8], both[:, 8:] + shift.reshape(GROUPS, 8, LANES)], axis=1).astype(BF)
    for k, (dx, dy, dz) in enumerate(OFFSETS):
        send(sum_out.at[ys[dy], xs[dx] + zs[dz]], sum_in.at[k], send_sem.at[7],
             recv_sem.at[7], chip(dx, dy, dz)).start()
    bo_turned[...] = bo_full[...].T
    final = sum_out[owner, group].astype(F32)
    finish(7, sum_in)
    for k in range(len(OFFSETS)):
        final = final + sum_in[k].astype(F32)

    final = final * (1.0 / total_samples)
    moments = final[0:8]
    ratio = final[8:16] / (moments + DAMPING)
    swap_out[...] = jnp.concatenate([ratio, moments], axis=0)
    swap = send(swap_out, swap_in, send_sem.at[8], recv_sem.at[8], twin)
    swap.start()
    swap.wait()
    mine, other = swap_out[...], swap_in[...]
    upper = jnp.where(core == 0, mine, other)
    lower = jnp.where(core == 0, other, mine)
    ring[owner, group] = jnp.concatenate([upper[0:8], lower[0:8]], axis=0).astype(BF)
    moments_ring[group] = jnp.concatenate([upper[8:16], lower[8:16]], axis=0).astype(BF)
    tile = ring.at[owner, group]
    for dx, dy, dz in OFFSETS:
        send(tile, tile, send_sem.at[9], recv_sem.at[9], chip(dx, dy, dz)).start()
    tile = moments_ring.at[group]
    for dx, dy, dz in OFFSETS:
        if dy == 0:
            send(tile, tile, send_sem.at[10], recv_sem.at[10], chip(dx, dy, dz)).start()
    ring_all = send(sum_in, sum_in, send_sem.at[9], recv_sem.at[9], twin)
    stat_all = moments_ring.at[pl.ds(0, GROUPS - 1)]
    stat_all = send(stat_all, stat_all, send_sem.at[10], recv_sem.at[10], twin)
    ring_all.wait_recv()

    ratios = jnp.concatenate(
        [ring[o].reshape(channels, LANES) for o in range(OWNERS)], axis=1)
    mixed = dot_nn(bo_turned[...], ratios).astype(BF)
    raw = dot_nt(mixed, bi_full[...])
    for o in range(OWNERS):
        raw_buf[o] = raw[:, o * LANES:(o + 1) * LANES]
    squares = jnp.sum(jnp.sum(raw * raw, axis=0, keepdims=True), axis=1, keepdims=True)
    mean_sq = squares * (1.0 / (channels * 2 * channels))
    update_ref[...] = raw_buf[owner] / jnp.sqrt(mean_sq + 1e-06)
    stat_all.wait_recv()
    stats_ref[...] = moments_ring[...].reshape(channels, LANES).astype(F32)
    ring_all.wait_send()
    stat_all.wait_send()


def copy_kernel(a_ref, b_ref, a_out, b_out):
    a_out[...] = a_ref[...]
    b_out[...] = b_ref[...]


def body(
    block_input_rows, spin_values, conv_weight, conv_bias, readout, energies, basis_out, basis_in
):
    samples, sites, channels = block_input_rows.shape
    vmem = pl.BlockSpec(memory_space=pltpu.VMEM)
    anywhere = pl.BlockSpec(memory_space=pl.ANY)
    dma = pltpu.SemaphoreType.DMA
    result = jax.ShapeDtypeStruct((channels, LANES), F32)
    pairs = pl.pallas_call(
        kernel,
        out_shape=(result, result),
        in_specs=[anywhere] * 5 + [pl.BlockSpec(memory_space=pltpu.SMEM)] + [anywhere] * 2,
        out_specs=(vmem, vmem),
        scratch_shapes=[
            pltpu.VMEM((samples, sites + DILATION_STEP, channels), BF),
            pltpu.VMEM((samples, sites), jnp.int32),
            pltpu.VMEM((1, channels), F32),
            pltpu.VMEM((1, channels), F32),
            pltpu.VMEM((channels, sites), BF),
            pltpu.VMEM((channels, sites), BF),
            pltpu.VMEM((samples, channels, 2 * channels), BF),
            pltpu.VMEM((samples, channels, 2 * channels), BF),
            pltpu.VMEM((channels, channels), BF),
            pltpu.VMEM((channels, channels), BF),
            pltpu.VMEM((channels, channels), BF),
            pltpu.VMEM((2 * channels, 2 * channels), BF),
            pltpu.VMEM((channels, LANES), F32),
            pltpu.VMEM((channels, LANES), F32),
            pltpu.VMEM((channels + 16, 2 * channels), BF),
            pltpu.VMEM((4, 8, LANES), F32),
            pltpu.VMEM((13, 8, LANES), F32),
            pltpu.VMEM((OWNERS, GROUPS, 16, LANES), BF),
            pltpu.VMEM((OWNERS, GROUPS, 16, LANES), BF),
            pltpu.VMEM((OWNERS, GROUPS, 16, LANES), F32),
            pltpu.VMEM((OWNERS, channels // 2, LANES), BF),
            pltpu.VMEM((OWNERS, channels // 2, LANES), BF),
            pltpu.VMEM((OWNERS, channels // 2, LANES), F32),
            pltpu.VMEM((OWNERS, GROUPS, 16, LANES), BF),
            pltpu.VMEM((len(OFFSETS), 16, LANES), BF),
            pltpu.VMEM((16, LANES), F32),
            pltpu.VMEM((16, LANES), F32),
            pltpu.VMEM((OWNERS, GROUPS, 16, LANES), BF),
            pltpu.VMEM((GROUPS, 16, LANES), BF),
            pltpu.VMEM((OWNERS, channels, LANES), F32),
            dma((samples // 2,)), dma((6,)), dma((12,)), dma((12,)),
        ],
        compiler_params=pltpu.CompilerParams(
            collective_id=0, has_side_effects=True, vmem_limit_bytes=56 << 20),
    )(
        block_input_rows, spin_values, conv_weight,
        conv_bias.reshape(1, channels), readout.reshape(1, channels), energies,
        basis_out.T, basis_in,
    )
    return pl.pallas_call(
        copy_kernel,
        out_shape=(result, result),
        in_specs=[vmem, vmem],
        out_specs=(vmem, vmem),
    )(*pairs)


def solution(mesh):
    in_specs = (
        P(("walker", "owner"), None, None),
        P(("walker", "owner"), None),
        P(),
        P(),
        P(),
        P(("walker", "owner")),
        P(None, "owner"),
        P(None, "owner"),
    )
    out_specs = (P(None, "owner"), P(None, "owner"))
    return jax.shard_map(body, mesh=mesh, in_specs=in_specs, out_specs=out_specs, check_vma=False)
```

```python
import jax
import jax.numpy as jnp
from jax import lax
from jax.experimental import pallas as pl
from jax.experimental.pallas import tpu as pltpu
from jax.sharding import PartitionSpec as P

DILATION_STEP = 16
DAMPING = 0.01
BF = jnp.bfloat16
F32 = jnp.float32
MESH = pl.DeviceIdType.MESH

GROUPS = 16
OWNERS = 4
LANES = 128


def dot_nt(a, b):
    return lax.dot_general(a, b, (((1,), (1,)), ((), ())), preferred_element_type=F32)


def dot_nn(a, b):
    return jnp.dot(a, b, preferred_element_type=F32)


def wide(value, count):
    return jnp.concatenate([value] * count, axis=1) if count > 1 else value


OFFSETS = sorted(
    [(dx, dy, dz) for dx in range(4) for dy in range(4) for dz in range(4)][1:],
    key=lambda step: -sum(min(d, 4 - d) for d in step),
)


def kernel(
    x_hbm, spin_hbm, w_hbm, bias_hbm, readout_hbm, e_ref, bo_hbm, bi_hbm,
    stats_ref, update_ref,
    xbuf, spin_ref, bias_ref, readout_ref, back_a, back_b, grads, halves, bo_full, bo_used,
    bo_turned, bi_full, bias_col, read_col, weight,
    e_out, e_in, core_out, core_in, own, plain_out, plain_in, own_plain, sum_out, sum_in, swap_out, swap_in,
    ring, moments_ring, raw_buf,
    x_sem, in_sem, send_sem, recv_sem,
):
    samples, sites, channels = x_hbm.shape
    pad = DILATION_STEP
    total_samples = samples * 128
    walker = lax.axis_index("walker")
    owner = lax.axis_index("owner")
    core = lax.rem(walker, 2)
    group = walker // 2
    gx, gz = group // 4, lax.rem(group, 4)
    xs = [gx * 4] + [lax.rem(gx + d, 4) * 4 for d in (1, 2, 3)]
    zs = [gz] + [lax.rem(gz + d, 4) for d in (1, 2, 3)]
    ys = [owner] + [lax.rem(owner + d, 4) for d in (1, 2, 3)]

    def chip(dx, dy, dz):
        return ((xs[dx] + zs[dz]) * 2 + core, ys[dy])

    twin = (group * 2 + (1 - core), owner)
    across = [((gx * 4 + gz) * 2 + 1 - core, ys[d]) for d in (1, 2, 3)]
    line_x = [chip(d, 0, 0) for d in (1, 2, 3)]
    line_y = [chip(0, d, 0) for d in (1, 2, 3)] + across + [twin]
    line_z = [chip(0, 0, d) for d in (1, 2, 3)]
    peers = line_x + line_z + line_y

    barrier = pltpu.get_barrier_semaphore()
    for peer in peers:
        pl.semaphore_signal(barrier, inc=1, device_id=peer, device_id_type=MESH)

    def load(j):
        pair = pl.ds(2 * j, 2)
        return pltpu.make_async_copy(
            x_hbm.at[pair], xbuf.at[pair, pl.ds(pad, sites), :], x_sem.at[j])

    own_rows = pl.ds(pl.multiple_of(owner * 64, 64), 64)
    own_cols = pl.ds(pl.multiple_of(owner * LANES, LANES), LANES)
    inputs = [
        pltpu.make_async_copy(w_hbm, weight.at[pl.ds(0, channels), :], in_sem.at[0]),
        pltpu.make_async_copy(bias_hbm, bias_ref, in_sem.at[1]),
        pltpu.make_async_copy(readout_hbm, readout_ref, in_sem.at[2]),
        pltpu.make_async_copy(spin_hbm, spin_ref, in_sem.at[3]),
    ]
    bases = [
        pltpu.make_async_copy(bo_hbm, bo_full.at[own_rows, :], in_sem.at[4]),
        pltpu.make_async_copy(bi_hbm, bi_full.at[:, own_cols], in_sem.at[5]),
    ]
    load(0).start()
    for c in inputs:
        c.start()
    for i in range(samples):
        xbuf[i, 0:pad, :] = jnp.zeros((pad, channels), BF)
    for c in inputs[1:3]:
        c.wait()

    def send(src, dst, ssem, rsem, peer):
        return pltpu.make_async_remote_copy(
            src_ref=src, dst_ref=dst, send_sem=ssem, recv_sem=rsem,
            device_id=peer, device_id_type=MESH,
        )

    bias_col[...] = jnp.broadcast_to(bias_ref[...], (LANES, channels)).T
    read_col[...] = jnp.broadcast_to(readout_ref[...], (LANES, channels)).T
    r = readout_ref[...]
    hi = r.astype(BF).astype(F32)
    mid = (r - hi).astype(BF).astype(F32)
    low = r - hi - mid
    row = lax.broadcasted_iota(jnp.int32, (16, channels), 0)
    spread = jnp.where(row == 0, hi, jnp.where(row == 1, mid, jnp.where(row == 2, low, 0.0)))
    weight[channels:, :channels] = jnp.zeros((16, channels), BF)
    weight[channels:, channels:] = spread.astype(BF)
    inputs[0].wait()
    inputs[3].wait()
    for j in range(1, samples // 2):
        load(j).start()
    for c in bases:
        c.start()

    bi_half = pl.ds(pl.multiple_of(core * channels, channels), channels)

    def bo_copies():
        part = bo_full.at[own_rows, :]
        return [send(part, part, send_sem.at[0], recv_sem.at[0], chip(0, d, 0))
                for d in (1, 2, 3)]

    def bi_copies():
        part = bi_full.at[bi_half, own_cols]
        return [send(part, part, send_sem.at[1], recv_sem.at[1], chip(0, d, 0))
                for d in (1, 2, 3)]

    def bi_relays():
        out = []
        for d in (1, 2, 3):
            cols = pl.ds(pl.multiple_of(ys[d] * LANES, LANES), LANES)
            part = bi_full.at[bi_half, cols]
            out.append(send(part, part, send_sem.at[2], recv_sem.at[2], twin))
        return out

    bo_all = bo_full.at[pl.ds(0, 192), :]
    bi_all = bi_full.at[pl.ds(0, channels), pl.ds(0, 3 * LANES)]

    def finish(k, part):
        both = send(part, part, send_sem.at[k], recv_sem.at[k], twin)
        both.wait_recv()
        both.wait_send()

    e_sum = e_ref[0]
    for i in range(1, samples):
        e_sum = e_sum + e_ref[i]
    e_out[0] = jnp.full((8, LANES), e_sum, F32)
    stages = [line_y, line_x, line_z]
    first_slot = [0, 7, 10]

    def energy_start(stage):
        for k, peer in enumerate(stages[stage]):
            send(e_out.at[stage], e_in.at[first_slot[stage] + k], send_sem.at[3 + stage],
                 recv_sem.at[3 + stage], peer).start()

    def energy_finish(stage):
        slots = range(first_slot[stage], first_slot[stage] + len(stages[stage]))
        finish(3 + stage, e_in.at[pl.ds(slots[0], len(slots))])
        total = e_out[stage]
        for k in slots:
            total = total + e_in[k]
        e_out[stage + 1] = total

    chunk = 256

    def forward(i, back):
        for c in range(sites // chunk):
            lo = c * chunk
            x_prev = xbuf[i, lo:lo + chunk, :]
            x_now = xbuf[i, lo + pad:lo + pad + chunk, :]
            out = dot_nt(weight[...], jnp.concatenate([x_prev, x_now], axis=1))
            act = jnp.tanh(out[:channels] + wide(bias_col[...], chunk // LANES))
            logit = jnp.sum(act * wide(read_col[...], chunk // LANES), axis=0, keepdims=True)
            logit = logit + jnp.sum(out[channels:], axis=0, keepdims=True)
            target = spin_ref[pl.ds(i, 1), lo:lo + chunk].astype(F32)
            signal = 0.5 * (target - jax.nn.sigmoid(logit))
            back[:, lo:lo + chunk] = (signal * (1.0 - act * act)).astype(BF)

    def gradient(i, back):
        scale = wide(read_col[...], channels // LANES)
        b = back[...]
        grads[i, :, :channels] = (dot_nn(b, xbuf[i, :sites, :]) * scale).astype(BF)
        grads[i, :, channels:] = (dot_nn(b, xbuf[i, pad:, :]) * scale).astype(BF)

    @pl.loop(0, samples // 2)
    def _(j):
        @pl.when(j == 2)
        def _():
            pl.semaphore_wait(barrier, len(peers))
            energy_start(0)
            for c in bases:
                c.wait()
            for c in bo_copies() + bi_copies():
                c.start()

        @pl.when(j == 5)
        def _():
            energy_finish(0)
            energy_start(1)

        load(j).wait()
        forward(2 * j, back_a)
        forward(2 * j + 1, back_b)
        gradient(2 * j, back_a)
        gradient(2 * j + 1, back_b)

    energy_finish(1)
    energy_start(2)
    finish(0, bo_all)
    finish(1, bi_all)
    for c in bi_relays():
        c.start()

    blocks = bo_full[...].astype(F32).reshape(GROUPS, 2, 8, channels)
    bo_used[...] = jnp.concatenate(
        [blocks[:, k].reshape(128, channels) for k in range(2)], axis=0).astype(BF)

    @pl.loop(0, samples // 8)
    def _(j):
        for u in range(8):
            halves[8 * j + u] = dot_nn(bo_used[...], grads[8 * j + u]).astype(BF)

    finish(2, bi_all)

    e_local = e_sum * (1.0 / samples)

    def project(first, tile):
        q, m = tile // 2, tile % 2
        rows = pl.ds(pl.multiple_of(first + q * 64, 64), 64)
        lhs = halves[:, rows, :].reshape(samples * 64, 2 * channels)
        p = dot_nn(lhs, bi_full[:, m * 256:(m + 1) * 256])
        squares = jnp.zeros((64, 256), F32)
        weighted = jnp.zeros((64, 256), F32)
        plain = jnp.zeros((64, 256), F32)
        for n in range(samples):
            pn = p[n * 64:(n + 1) * 64]
            squares = squares + pn * pn
            weighted = weighted + pn * (e_ref[n] - e_local)
            plain = plain + pn
        out = []
        for k in range(2):
            cols = slice(k * LANES, (k + 1) * LANES)
            parts = [v[:, cols].reshape(8, 8, LANES) for v in (squares, weighted)]
            out.append((2 * m + k, q, jnp.concatenate(parts, axis=1), plain[:, cols]))
        return out

    for tile in range(4):
        for o, q, block, plain in project((1 - core) * 128, tile):
            core_out[o, q * 8:q * 8 + 8] = block.astype(BF)
            plain_out[o, q * 64:q * 64 + 64] = plain.astype(BF)
        if tile % 2:
            q = tile // 2
            part = pl.ds(q * 8, 8)
            send(core_out.at[:, part], core_in.at[:, part], send_sem.at[6], recv_sem.at[6],
                 twin).start()
            part = pl.ds(q * 64, 64)
            send(plain_out.at[:, part], plain_in.at[:, part], send_sem.at[11], recv_sem.at[11],
                 twin).start()
    for tile in range(4):
        for o, q, block, plain in project(core * 128, tile):
            own[o, q * 8:q * 8 + 8] = block
            own_plain[o, q * 64:q * 64 + 64] = plain
    energy_finish(2)
    e_mean = e_out[3][0:1, :] * (1.0 / total_samples)
    here = e_out[0][0:1, :] * (1.0 / samples) - e_mean
    there = e_in[6][0:1, :] * (1.0 / samples) - e_mean
    finish(6, core_in)
    finish(11, plain_in)

    for step in (2, 1, 3, 0):
        o = ys[step]
        both = own[o] + core_in[o].astype(F32)
        shift = own_plain[o] * here + plain_in[o].astype(F32) * there
        sum_out[o] = jnp.concatenate(
            [both[:, :8], both[:, 8:] + shift.reshape(GROUPS, 8, LANES)], axis=1).astype(BF)
        for k, (dx, dy, dz) in enumerate(OFFSETS):
            if dy == step:
                send(sum_out.at[o, xs[dx] + zs[dz]], sum_in.at[k], send_sem.at[7],
                     recv_sem.at[7], chip(dx, dy, dz)).start()
    bo_turned[...] = bo_full[...].T
    final = sum_out[owner, group].astype(F32)
    finish(7, sum_in)
    for k in range(len(OFFSETS)):
        final = final + sum_in[k].astype(F32)

    final = final * (1.0 / total_samples)
    moments = final[0:8]
    ratio = final[8:16] / (moments + DAMPING)
    swap_out[...] = jnp.concatenate([ratio, moments], axis=0)
    swap = send(swap_out, swap_in, send_sem.at[8], recv_sem.at[8], twin)
    swap.start()
    swap.wait()
    mine, other = swap_out[...], swap_in[...]
    upper = jnp.where(core == 0, mine, other)
    lower = jnp.where(core == 0, other, mine)
    ring[owner, group] = jnp.concatenate([upper[0:8], lower[0:8]], axis=0).astype(BF)
    moments_ring[group] = jnp.concatenate([upper[8:16], lower[8:16]], axis=0).astype(BF)
    tile = ring.at[owner, group]
    for dx, dy, dz in OFFSETS:
        send(tile, tile, send_sem.at[9], recv_sem.at[9], chip(dx, dy, dz)).start()
    tile = moments_ring.at[group]
    for dx, dy, dz in OFFSETS:
        if dy == 0:
            send(tile, tile, send_sem.at[10], recv_sem.at[10], chip(dx, dy, dz)).start()
    ring_all = send(sum_in, sum_in, send_sem.at[9], recv_sem.at[9], twin)
    stat_all = moments_ring.at[pl.ds(0, GROUPS - 1)]
    stat_all = send(stat_all, stat_all, send_sem.at[10], recv_sem.at[10], twin)
    ring_all.wait_recv()

    ratios = jnp.concatenate(
        [ring[o].reshape(channels, LANES) for o in range(OWNERS)], axis=1)
    mixed = dot_nn(bo_turned[...], ratios).astype(BF)
    raw = dot_nt(mixed, bi_full[...])
    for o in range(OWNERS):
        raw_buf[o] = raw[:, o * LANES:(o + 1) * LANES]
    squares = jnp.sum(jnp.sum(raw * raw, axis=0, keepdims=True), axis=1, keepdims=True)
    mean_sq = squares * (1.0 / (channels * 2 * channels))
    update_ref[...] = raw_buf[owner] / jnp.sqrt(mean_sq + 1e-06)
    stat_all.wait_recv()
    stats_ref[...] = moments_ring[...].reshape(channels, LANES).astype(F32)
    ring_all.wait_send()
    stat_all.wait_send()


def copy_kernel(a_ref, b_ref, a_out, b_out):
    a_out[...] = a_ref[...]
    b_out[...] = b_ref[...]


def body(
    block_input_rows, spin_values, conv_weight, conv_bias, readout, energies, basis_out, basis_in
):
    samples, sites, channels = block_input_rows.shape
    vmem = pl.BlockSpec(memory_space=pltpu.VMEM)
    anywhere = pl.BlockSpec(memory_space=pl.ANY)
    dma = pltpu.SemaphoreType.DMA
    result = jax.ShapeDtypeStruct((channels, LANES), F32)
    kept = pltpu.VMEM((channels, LANES), F32)
    pairs = pl.pallas_call(
        kernel,
        out_shape=(kept, kept),
        in_specs=[anywhere] * 5 + [pl.BlockSpec(memory_space=pltpu.SMEM)] + [anywhere] * 2,
        out_specs=(vmem, vmem),
        scratch_shapes=[
            pltpu.VMEM((samples, sites + DILATION_STEP, channels), BF),
            pltpu.VMEM((samples, sites), jnp.int32),
            pltpu.VMEM((1, channels), F32),
            pltpu.VMEM((1, channels), F32),
            pltpu.VMEM((channels, sites), BF),
            pltpu.VMEM((channels, sites), BF),
            pltpu.VMEM((samples, channels, 2 * channels), BF),
            pltpu.VMEM((samples, channels, 2 * channels), BF),
            pltpu.VMEM((channels, channels), BF),
            pltpu.VMEM((channels, channels), BF),
            pltpu.VMEM((channels, channels), BF),
            pltpu.VMEM((2 * channels, 2 * channels), BF),
            pltpu.VMEM((channels, LANES), F32),
            pltpu.VMEM((channels, LANES), F32),
            pltpu.VMEM((channels + 16, 2 * channels), BF),
            pltpu.VMEM((4, 8, LANES), F32),
            pltpu.VMEM((13, 8, LANES), F32),
            pltpu.VMEM((OWNERS, GROUPS, 16, LANES), BF),
            pltpu.VMEM((OWNERS, GROUPS, 16, LANES), BF),
            pltpu.VMEM((OWNERS, GROUPS, 16, LANES), F32),
            pltpu.VMEM((OWNERS, channels // 2, LANES), BF),
            pltpu.VMEM((OWNERS, channels // 2, LANES), BF),
            pltpu.VMEM((OWNERS, channels // 2, LANES), F32),
            pltpu.VMEM((OWNERS, GROUPS, 16, LANES), BF),
            pltpu.VMEM((len(OFFSETS), 16, LANES), BF),
            pltpu.VMEM((16, LANES), F32),
            pltpu.VMEM((16, LANES), F32),
            pltpu.VMEM((OWNERS, GROUPS, 16, LANES), BF),
            pltpu.VMEM((GROUPS, 16, LANES), BF),
            pltpu.VMEM((OWNERS, channels, LANES), F32),
            dma((samples // 2,)), dma((6,)), dma((12,)), dma((12,)),
        ],
        compiler_params=pltpu.CompilerParams(
            collective_id=0, has_side_effects=True, vmem_limit_bytes=56 << 20),
    )(
        block_input_rows, spin_values, conv_weight,
        conv_bias.reshape(1, channels), readout.reshape(1, channels), energies,
        basis_out.T, basis_in,
    )
    return pl.pallas_call(
        copy_kernel,
        out_shape=(result, result),
        in_specs=[vmem, vmem],
        out_specs=(vmem, vmem),
    )(*[pltpu.with_memory_space_constraint(p, pltpu.VMEM) for p in pairs])


def solution(mesh):
    in_specs = (
        P(("walker", "owner"), None, None),
        P(("walker", "owner"), None),
        P(),
        P(),
        P(),
        P(("walker", "owner")),
        P(None, "owner"),
        P(None, "owner"),
    )
    out_specs = (P(None, "owner"), P(None, "owner"))
    return jax.shard_map(body, mesh=mesh, in_specs=in_specs, out_specs=out_specs, check_vma=False)
```

```python
import jax
import jax.numpy as jnp
from jax import lax
from jax.experimental import pallas as pl
from jax.experimental.pallas import tpu as pltpu
from jax.sharding import PartitionSpec as P

DILATION_STEP = 16
DAMPING = 0.01
BF = jnp.bfloat16
F32 = jnp.float32
MESH = pl.DeviceIdType.MESH

GROUPS = 16
OWNERS = 4
LANES = 128


def dot_nt(a, b):
    return lax.dot_general(a, b, (((1,), (1,)), ((), ())), preferred_element_type=F32)


def dot_nn(a, b):
    return jnp.dot(a, b, preferred_element_type=F32)


def wide(value, count):
    return jnp.concatenate([value] * count, axis=1) if count > 1 else value


OFFSETS = sorted(
    [(dx, dy, dz) for dx in range(4) for dy in range(4) for dz in range(4)][1:],
    key=lambda step: -sum(min(d, 4 - d) for d in step),
)


def kernel(
    x_hbm, spin_hbm, w_hbm, bias_hbm, readout_hbm, e_ref, bo_hbm, bi_hbm,
    stats_ref, update_ref,
    xbuf, spin_ref, bias_ref, readout_ref, back_a, back_b, grads, halves, bo_full, bo_used,
    bo_turned, bi_full, bias_col, read_col, weight,
    e_out, e_in, core_out, core_in, own, plain_out, plain_in, own_plain, sum_out, sum_in, swap_out, swap_in,
    ring, moments_ring, raw_buf,
    x_sem, in_sem, send_sem, recv_sem,
):
    samples, sites, channels = x_hbm.shape
    pad = DILATION_STEP
    total_samples = samples * 128
    walker = lax.axis_index("walker")
    owner = lax.axis_index("owner")
    core = lax.rem(walker, 2)
    group = walker // 2
    gx, gz = group // 4, lax.rem(group, 4)
    xs = [gx * 4] + [lax.rem(gx + d, 4) * 4 for d in (1, 2, 3)]
    zs = [gz] + [lax.rem(gz + d, 4) for d in (1, 2, 3)]
    ys = [owner] + [lax.rem(owner + d, 4) for d in (1, 2, 3)]

    def chip(dx, dy, dz):
        return ((xs[dx] + zs[dz]) * 2 + core, ys[dy])

    twin = (group * 2 + (1 - core), owner)
    across = [((gx * 4 + gz) * 2 + 1 - core, ys[d]) for d in (1, 2, 3)]
    line_x = [chip(d, 0, 0) for d in (1, 2, 3)]
    line_y = [chip(0, d, 0) for d in (1, 2, 3)] + across + [twin]
    line_z = [chip(0, 0, d) for d in (1, 2, 3)]
    peers = line_x + line_z + line_y

    barrier = pltpu.get_barrier_semaphore()
    for peer in peers:
        pl.semaphore_signal(barrier, inc=1, device_id=peer, device_id_type=MESH)

    def load(j):
        pair = pl.ds(2 * j, 2)
        return pltpu.make_async_copy(
            x_hbm.at[pair], xbuf.at[pair, pl.ds(pad, sites), :], x_sem.at[j])

    own_rows = pl.ds(pl.multiple_of(owner * 64, 64), 64)
    own_cols = pl.ds(pl.multiple_of(owner * LANES, LANES), LANES)
    inputs = [
        pltpu.make_async_copy(w_hbm, weight.at[pl.ds(0, channels), :], in_sem.at[0]),
        pltpu.make_async_copy(bias_hbm, bias_ref, in_sem.at[1]),
        pltpu.make_async_copy(readout_hbm, readout_ref, in_sem.at[2]),
        pltpu.make_async_copy(spin_hbm, spin_ref, in_sem.at[3]),
    ]
    bases = [
        pltpu.make_async_copy(bo_hbm, bo_full.at[own_rows, :], in_sem.at[4]),
        pltpu.make_async_copy(bi_hbm, bi_full.at[:, own_cols], in_sem.at[5]),
    ]
    load(0).start()
    for c in inputs:
        c.start()
    for i in range(samples):
        xbuf[i, 0:pad, :] = jnp.zeros((pad, channels), BF)
    for c in inputs[1:3]:
        c.wait()

    def send(src, dst, ssem, rsem, peer):
        return pltpu.make_async_remote_copy(
            src_ref=src, dst_ref=dst, send_sem=ssem, recv_sem=rsem,
            device_id=peer, device_id_type=MESH,
        )

    bias_col[...] = jnp.broadcast_to(bias_ref[...], (LANES, channels)).T
    read_col[...] = jnp.broadcast_to(readout_ref[...], (LANES, channels)).T
    r = readout_ref[...]
    hi = r.astype(BF).astype(F32)
    mid = (r - hi).astype(BF).astype(F32)
    low = r - hi - mid
    row = lax.broadcasted_iota(jnp.int32, (16, channels), 0)
    spread = jnp.where(row == 0, hi, jnp.where(row == 1, mid, jnp.where(row == 2, low, 0.0)))
    weight[channels:, :channels] = jnp.zeros((16, channels), BF)
    weight[channels:, channels:] = spread.astype(BF)
    inputs[0].wait()
    inputs[3].wait()
    for j in range(1, samples // 2):
        load(j).start()
    for c in bases:
        c.start()

    bi_half = pl.ds(pl.multiple_of(core * channels, channels), channels)

    def bo_copies():
        part = bo_full.at[own_rows, :]
        return [send(part, part, send_sem.at[0], recv_sem.at[0], chip(0, d, 0))
                for d in (1, 2, 3)]

    def bi_copies():
        part = bi_full.at[bi_half, own_cols]
        return [send(part, part, send_sem.at[1], recv_sem.at[1], chip(0, d, 0))
                for d in (1, 2, 3)]

    def bi_relays():
        out = []
        for d in (1, 2, 3):
            cols = pl.ds(pl.multiple_of(ys[d] * LANES, LANES), LANES)
            part = bi_full.at[bi_half, cols]
            out.append(send(part, part, send_sem.at[2], recv_sem.at[2], twin))
        return out

    bo_all = bo_full.at[pl.ds(0, 192), :]
    bi_all = bi_full.at[pl.ds(0, channels), pl.ds(0, 3 * LANES)]

    def finish(k, part):
        both = send(part, part, send_sem.at[k], recv_sem.at[k], twin)
        both.wait_recv()
        both.wait_send()

    e_sum = e_ref[0]
    for i in range(1, samples):
        e_sum = e_sum + e_ref[i]
    e_out[0] = jnp.full((8, LANES), e_sum, F32)
    stages = [line_y, line_x, line_z]
    first_slot = [0, 7, 10]

    def energy_start(stage):
        for k, peer in enumerate(stages[stage]):
            send(e_out.at[stage], e_in.at[first_slot[stage] + k], send_sem.at[3 + stage],
                 recv_sem.at[3 + stage], peer).start()

    def energy_finish(stage):
        slots = range(first_slot[stage], first_slot[stage] + len(stages[stage]))
        finish(3 + stage, e_in.at[pl.ds(slots[0], len(slots))])
        total = e_out[stage]
        for k in slots:
            total = total + e_in[k]
        e_out[stage + 1] = total

    chunk = 256

    def forward(i, back):
        for c in range(sites // chunk):
            lo = c * chunk
            x_prev = xbuf[i, lo:lo + chunk, :]
            x_now = xbuf[i, lo + pad:lo + pad + chunk, :]
            out = dot_nt(weight[...], jnp.concatenate([x_prev, x_now], axis=1))
            act = jnp.tanh(out[:channels] + wide(bias_col[...], chunk // LANES))
            logit = jnp.sum(act * wide(read_col[...], chunk // LANES), axis=0, keepdims=True)
            logit = logit + jnp.sum(out[channels:], axis=0, keepdims=True)
            target = spin_ref[pl.ds(i, 1), lo:lo + chunk].astype(F32)
            signal = 0.5 * (target - jax.nn.sigmoid(logit))
            back[:, lo:lo + chunk] = (signal * (1.0 - act * act)).astype(BF)

    def gradient(i, back):
        scale = wide(read_col[...], channels // LANES)
        b = back[...]
        grads[i, :, :channels] = (dot_nn(b, xbuf[i, :sites, :]) * scale).astype(BF)
        grads[i, :, channels:] = (dot_nn(b, xbuf[i, pad:, :]) * scale).astype(BF)

    @pl.loop(0, samples // 2)
    def _(j):
        @pl.when(j == 2)
        def _():
            pl.semaphore_wait(barrier, len(peers))
            energy_start(0)
            for c in bases:
                c.wait()
            for c in bo_copies() + bi_copies():
                c.start()

        @pl.when(j == 5)
        def _():
            energy_finish(0)
            energy_start(1)

        load(j).wait()
        forward(2 * j, back_a)
        forward(2 * j + 1, back_b)
        gradient(2 * j, back_a)
        gradient(2 * j + 1, back_b)

    energy_finish(1)
    energy_start(2)
    finish(0, bo_all)
    finish(1, bi_all)
    for c in bi_relays():
        c.start()

    blocks = bo_full[...].astype(F32).reshape(GROUPS, 2, 8, channels)
    bo_used[...] = jnp.concatenate(
        [blocks[:, k].reshape(128, channels) for k in range(2)], axis=0).astype(BF)

    @pl.loop(0, samples // 8)
    def _(j):
        for u in range(8):
            halves[8 * j + u] = dot_nn(bo_used[...], grads[8 * j + u]).astype(BF)

    finish(2, bi_all)

    e_local = e_sum * (1.0 / samples)

    def project(first, tile):
        q, m = tile // 2, tile % 2
        rows = pl.ds(pl.multiple_of(first + q * 64, 64), 64)
        lhs = halves[:, rows, :].reshape(samples * 64, 2 * channels)
        p = dot_nn(lhs, bi_full[:, m * 256:(m + 1) * 256])
        squares = jnp.zeros((64, 256), F32)
        weighted = jnp.zeros((64, 256), F32)
        plain = jnp.zeros((64, 256), F32)
        for n in range(samples):
            pn = p[n * 64:(n + 1) * 64]
            squares = squares + pn * pn
            weighted = weighted + pn * (e_ref[n] - e_local)
            plain = plain + pn
        out = []
        for k in range(2):
            cols = slice(k * LANES, (k + 1) * LANES)
            parts = [v[:, cols].reshape(8, 8, LANES) for v in (squares, weighted)]
            out.append((2 * m + k, q, jnp.concatenate(parts, axis=1), plain[:, cols]))
        return out

    for tile in range(4):
        for o, q, block, plain in project((1 - core) * 128, tile):
            core_out[o, q * 8:q * 8 + 8] = block.astype(BF)
            plain_out[o, q * 64:q * 64 + 64] = plain.astype(BF)
        if tile % 2:
            q = tile // 2
            part = pl.ds(q * 8, 8)
            send(core_out.at[:, part], core_in.at[:, part], send_sem.at[6], recv_sem.at[6],
                 twin).start()
            part = pl.ds(q * 64, 64)
            send(plain_out.at[:, part], plain_in.at[:, part], send_sem.at[11], recv_sem.at[11],
                 twin).start()
    for tile in range(4):
        for o, q, block, plain in project(core * 128, tile):
            own[o, q * 8:q * 8 + 8] = block
            own_plain[o, q * 64:q * 64 + 64] = plain
    energy_finish(2)
    e_mean = e_out[3][0:1, :] * (1.0 / total_samples)
    here = e_out[0][0:1, :] * (1.0 / samples) - e_mean
    there = e_in[6][0:1, :] * (1.0 / samples) - e_mean
    finish(6, core_in)
    finish(11, plain_in)

    for step in (2, 1, 3, 0):
        o = ys[step]
        both = own[o] + core_in[o].astype(F32)
        shift = own_plain[o] * here + plain_in[o].astype(F32) * there
        sum_out[o] = jnp.concatenate(
            [both[:, :8], both[:, 8:] + shift.reshape(GROUPS, 8, LANES)], axis=1).astype(BF)
        for k, (dx, dy, dz) in enumerate(OFFSETS):
            if dy == step:
                send(sum_out.at[o, xs[dx] + zs[dz]], sum_in.at[k], send_sem.at[7],
                     recv_sem.at[7], chip(dx, dy, dz)).start()
    bo_turned[...] = bo_full[...].T
    final = sum_out[owner, group].astype(F32)
    finish(7, sum_in)
    for k in range(len(OFFSETS)):
        final = final + sum_in[k].astype(F32)

    final = final * (1.0 / total_samples)
    moments = final[0:8]
    ratio = final[8:16] / (moments + DAMPING)
    swap_out[...] = jnp.concatenate([ratio, moments], axis=0)
    swap = send(swap_out, swap_in, send_sem.at[8], recv_sem.at[8], twin)
    swap.start()
    swap.wait()
    mine, other = swap_out[...], swap_in[...]
    upper = jnp.where(core == 0, mine, other)
    lower = jnp.where(core == 0, other, mine)
    ring[owner, group] = jnp.concatenate([upper[0:8], lower[0:8]], axis=0).astype(BF)
    moments_ring[group] = jnp.concatenate([upper[8:16], lower[8:16]], axis=0).astype(BF)
    tile = ring.at[owner, group]
    for dx, dy, dz in OFFSETS:
        send(tile, tile, send_sem.at[9], recv_sem.at[9], chip(dx, dy, dz)).start()
    tile = moments_ring.at[group]
    for dx, dy, dz in OFFSETS:
        if dy == 0:
            send(tile, tile, send_sem.at[10], recv_sem.at[10], chip(dx, dy, dz)).start()
    ring_all = send(sum_in, sum_in, send_sem.at[9], recv_sem.at[9], twin)
    stat_all = moments_ring.at[pl.ds(0, GROUPS - 1)]
    stat_all = send(stat_all, stat_all, send_sem.at[10], recv_sem.at[10], twin)
    ring_all.wait_recv()

    ratios = jnp.concatenate(
        [ring[o].reshape(channels, LANES) for o in range(OWNERS)], axis=1)
    mixed = dot_nn(bo_turned[...], ratios).astype(BF)
    raw = dot_nt(mixed, bi_full[...])
    for o in range(OWNERS):
        raw_buf[o] = raw[:, o * LANES:(o + 1) * LANES]
    squares = jnp.sum(jnp.sum(raw * raw, axis=0, keepdims=True), axis=1, keepdims=True)
    mean_sq = squares * (1.0 / (channels * 2 * channels))
    update_ref[...] = raw_buf[owner] / jnp.sqrt(mean_sq + 1e-06)
    stat_all.wait_recv()
    stats_ref[...] = moments_ring[...].reshape(channels, LANES).astype(F32)
    ring_all.wait_send()
    stat_all.wait_send()


def copy_kernel(a_ref, b_ref, a_out, b_out, sems):
    first = pltpu.make_async_copy(a_ref, a_out, sems.at[0])
    second = pltpu.make_async_copy(b_ref, b_out, sems.at[1])
    first.start()
    second.start()
    first.wait()
    second.wait()


def body(
    block_input_rows, spin_values, conv_weight, conv_bias, readout, energies, basis_out, basis_in
):
    samples, sites, channels = block_input_rows.shape
    vmem = pl.BlockSpec(memory_space=pltpu.VMEM)
    anywhere = pl.BlockSpec(memory_space=pl.ANY)
    dma = pltpu.SemaphoreType.DMA
    result = jax.ShapeDtypeStruct((channels, LANES), F32)
    kept = pltpu.VMEM((channels, LANES), F32)
    pairs = pl.pallas_call(
        kernel,
        out_shape=(kept, kept),
        in_specs=[anywhere] * 5 + [pl.BlockSpec(memory_space=pltpu.SMEM)] + [anywhere] * 2,
        out_specs=(vmem, vmem),
        scratch_shapes=[
            pltpu.VMEM((samples, sites + DILATION_STEP, channels), BF),
            pltpu.VMEM((samples, sites), jnp.int32),
            pltpu.VMEM((1, channels), F32),
            pltpu.VMEM((1, channels), F32),
            pltpu.VMEM((channels, sites), BF),
            pltpu.VMEM((channels, sites), BF),
            pltpu.VMEM((samples, channels, 2 * channels), BF),
            pltpu.VMEM((samples, channels, 2 * channels), BF),
            pltpu.VMEM((channels, channels), BF),
            pltpu.VMEM((channels, channels), BF),
            pltpu.VMEM((channels, channels), BF),
            pltpu.VMEM((2 * channels, 2 * channels), BF),
            pltpu.VMEM((channels, LANES), F32),
            pltpu.VMEM((channels, LANES), F32),
            pltpu.VMEM((channels + 16, 2 * channels), BF),
            pltpu.VMEM((4, 8, LANES), F32),
            pltpu.VMEM((13, 8, LANES), F32),
            pltpu.VMEM((OWNERS, GROUPS, 16, LANES), BF),
            pltpu.VMEM((OWNERS, GROUPS, 16, LANES), BF),
            pltpu.VMEM((OWNERS, GROUPS, 16, LANES), F32),
            pltpu.VMEM((OWNERS, channels // 2, LANES), BF),
            pltpu.VMEM((OWNERS, channels // 2, LANES), BF),
            pltpu.VMEM((OWNERS, channels // 2, LANES), F32),
            pltpu.VMEM((OWNERS, GROUPS, 16, LANES), BF),
            pltpu.VMEM((len(OFFSETS), 16, LANES), BF),
            pltpu.VMEM((16, LANES), F32),
            pltpu.VMEM((16, LANES), F32),
            pltpu.VMEM((OWNERS, GROUPS, 16, LANES), BF),
            pltpu.VMEM((GROUPS, 16, LANES), BF),
            pltpu.VMEM((OWNERS, channels, LANES), F32),
            dma((samples // 2,)), dma((6,)), dma((12,)), dma((12,)),
        ],
        compiler_params=pltpu.CompilerParams(
            collective_id=0, has_side_effects=True, vmem_limit_bytes=56 << 20),
    )(
        block_input_rows, spin_values, conv_weight,
        conv_bias.reshape(1, channels), readout.reshape(1, channels), energies,
        basis_out.T, basis_in,
    )
    return pl.pallas_call(
        copy_kernel,
        out_shape=(result, result),
        in_specs=[vmem, vmem],
        out_specs=(anywhere, anywhere),
        scratch_shapes=[dma((2,))],
    )(*[pltpu.with_memory_space_constraint(p, pltpu.VMEM) for p in pairs])


def solution(mesh):
    in_specs = (
        P(("walker", "owner"), None, None),
        P(("walker", "owner"), None),
        P(),
        P(),
        P(),
        P(("walker", "owner")),
        P(None, "owner"),
        P(None, "owner"),
    )
    out_specs = (P(None, "owner"), P(None, "owner"))
    return jax.shard_map(body, mesh=mesh, in_specs=in_specs, out_specs=out_specs, check_vma=False)
```
